256 devices in a mesh: gen: 8 (over y, core), bus: 32 (over x, z).
Axes of the slice: x: 4, y: 4, z: 8, core: 2. Of those that a mesh axis runs over, the one named last changes fastest.
Arguments:
- bus_price: float32 [32, 12, 16384], P(None, None, 'bus'), may hold values from -4 to 4
- bus_demand: float32 [32, 12, 16384], P('gen', None, 'bus'), may hold values from 0 to 2
- multipliers: float32 [2, 32, 12, 24576], P(None, 'gen', None, 'bus'), may hold values from 0 to 1
- line_limits: float32 [24576], P('bus'), may hold values from 0.3 to 3
- ptdf_blocks: bfloat16 [192, 16, 128, 128], P('bus'), may hold values from -0.125 to 0.125
- ptdf_pattern: int32 [192, 16], P('bus'), may hold values from 0 to 127, as said below
- gen_bus: int32 [4096], P(('gen', 'bus')), may hold values from 0 to 16383, as said below
- state_counts: int32 [4096], P(('gen', 'bus')), may hold values from 64 to 512, as said below
- transitions: int32 [4096, 3, 512], P(('gen', 'bus')), may hold values from 0 to 511, as said below
- state_level: float32 [4096, 512], P(('gen', 'bus')), may hold values from 0 to 3
- state_cost: float32 [4096, 512], P(('gen', 'bus')), may hold values from 0 to 2
Outputs:
- new_multipliers: float32 [2, 32, 12, 24576], P(None, 'gen', None, 'bus')
- new_price: float32 [32, 12, 16384], P(None, None, 'bus')
The draws below stay inside these ranges and needn't reach their ends.
Inputs may be any that keep to these rules, and one draw needn't show every extreme that they name: Generator i sits in bus block (i // 16) % 32: gen_bus[i] // 512 equals that number. `state_counts`: among the generators of each aligned group of 16, at most 6 have a count above 256, and some group has exactly 6. `transitions`: every successor of a state below its generator's count is below that count; a state at or above the count has itself as every successor. `ptdf_pattern`: the 16 bus blocks named in one row are different.
All inputs are finite; a program needn't handle non-finite values.
Results may differ from the reference program's by a relative error of at most 0.0031.
Values may be sent and summed in bfloat16 or wider, within the bound.
A program may use at most 128 MiB of HBM per device.

```python
import math
import jax
import jax.numpy as jnp
from jax import lax

STATES = 512
SUCC = 3
HOURS = 12
GEN_DEV = 16
BIG_DEV = 6
BLK = 128
NNZB = 16
BUS_DEV = 512
SCN = 32
GENS = 4096
BUSES = 16384
LINES = 24576


def count_table(key):
    device_total = GENS // GEN_DEV
    subkeys = jax.random.split(jax.random.fold_in(key, 11), 5)
    big_number = jax.random.randint(subkeys[0], (device_total,), 0, BIG_DEV + 1)
    busiest = jax.random.randint(subkeys[1], (), 0, device_total)
    device_ids = jnp.arange(device_total, dtype=jnp.int32)
    big_number = jnp.where(device_ids == busiest, BIG_DEV, big_number)
    scores = jax.random.randint(subkeys[2], (device_total, GEN_DEV), 0, 1 << 20) * GEN_DEV + jnp.arange(GEN_DEV, dtype=jnp.int32)[None, :]
    rank_table = jnp.argsort(jnp.argsort(scores, axis=1), axis=1)
    large_counts = jax.random.randint(subkeys[3], (device_total, GEN_DEV), STATES // 2 + 1, STATES + 1)
    small_counts = jax.random.randint(subkeys[4], (device_total, GEN_DEV), STATES // 8, STATES // 2 + 1)
    counts = jnp.where(rank_table < big_number[:, None], large_counts, small_counts)
    on_busiest = (device_ids == busiest)[:, None]
    counts = jnp.where(on_busiest & (rank_table == 0), STATES, counts)
    counts = jnp.where(on_busiest & (rank_table == GEN_DEV - 1), STATES // 8, counts)
    return counts.reshape(GENS).astype(jnp.int32)


def draw_state_counts(key, part):
    return count_table(key)


def draw_transitions(key, part):
    counts = count_table(key)
    chosen = jax.random.randint(jax.random.fold_in(key, 12), (GENS, SUCC, STATES), 0, counts[:, None, None])
    state_ids = jnp.broadcast_to(jnp.arange(STATES, dtype=jnp.int32)[None, None, :], (GENS, SUCC, STATES))
    return jnp.where(state_ids < counts[:, None, None], chosen, state_ids).astype(jnp.int32)


def draw_gen_bus(key, part):
    gen_ids = jnp.arange(GENS, dtype=jnp.int32)
    block_ids = gen_ids // GEN_DEV % (BUSES // BUS_DEV)
    offsets = jax.random.randint(jax.random.fold_in(key, 14), (GENS,), 0, BUS_DEV)
    offsets = jnp.where(gen_ids == GENS - 1, BUS_DEV - 1, offsets)
    offsets = jnp.where(gen_ids == 0, 0, offsets)
    return (block_ids * BUS_DEV + offsets).astype(jnp.int32)


def draw_ptdf_pattern(key, part):
    block_total = BUSES // BLK
    line_total = LINES // BLK
    subkeys = jax.random.split(jax.random.fold_in(key, 15), line_total)

    def pick_row(row_key):
        return jax.random.permutation(row_key, block_total)[:NNZB]
    return jax.vmap(pick_row)(subkeys).astype(jnp.int32)


def block_levels(own_key, dims, shards, least, largest):
    level, own = 1.0, jax.random.fold_in(own_key, 6)
    for axis_at, parts in shards:
        steps = jnp.exp(jax.random.uniform(jax.random.fold_in(own, axis_at), (parts,), jnp.float32, least / len(shards), largest / len(shards)))
        level = level * jnp.repeat(steps, dims[axis_at] // parts).reshape([-1 if axis == axis_at else 1 for axis in range(len(dims))])
    return level


def scatter_about(stream_key, shape, scale, bound, pieces=(), kind=jnp.bfloat16):
    level = block_levels(stream_key, shape, pieces, -0.22, 0.18) if pieces else 1.0
    drawn = jax.random.normal(stream_key, shape, jnp.float32) * scale * level
    return jnp.minimum(jnp.maximum(drawn, -bound), bound).astype(kind)


def setup_inputs(seed: int = 0) -> dict:
    seeds = jax.random.split(jax.random.key(seed), 12)
    return {
        "bus_price": scatter_about(seeds[0], (SCN, HOURS, BUSES), 1.0, 4.0, ((2, 32),), jnp.float32),
        "bus_demand": jnp.clip(2.0 * jax.random.uniform(seeds[1], (SCN, HOURS, BUSES), jnp.float32) ** block_levels(seeds[1], (SCN, HOURS, BUSES), ((0, 8), (2, 32)), -0.2, 0.2), 0.0, 2.0),
        "multipliers": jnp.clip(1.0 * jax.random.uniform(seeds[2], (2, SCN, HOURS, LINES), jnp.float32) ** block_levels(seeds[2], (2, SCN, HOURS, LINES), ((1, 8), (3, 32)), -0.2, 0.2), 0.0, 1.0),
        "line_limits": jnp.clip(jnp.exp(math.log(3.0) - 2.3025851 * jax.random.uniform(seeds[3], (LINES,), jnp.float32) ** block_levels(seeds[3], (LINES,), ((0, 32),), -0.2, 0.2)), 0.3, 3.0),
        "ptdf_blocks": scatter_about(seeds[4], (LINES // BLK, NNZB, BLK, BLK), (NNZB * BLK) ** -0.5, 0.125, ((0, 32),)),
        "ptdf_pattern": draw_ptdf_pattern(jax.random.fold_in(seeds[11], 71), 0),
        "gen_bus": draw_gen_bus(jax.random.fold_in(seeds[11], 71), 0),
        "state_counts": draw_state_counts(jax.random.fold_in(seeds[11], 71), 0),
        "transitions": draw_transitions(jax.random.fold_in(seeds[11], 71), 0),
        "state_level": jnp.clip(3.0 * jax.random.uniform(seeds[9], (GENS, STATES), jnp.float32) ** block_levels(seeds[9], (GENS, STATES), ((0, 256),), -0.2, 0.2), 0.0, 3.0),
        "state_cost": jnp.clip(2.0 * jax.random.uniform(seeds[10], (GENS, STATES), jnp.float32) ** block_levels(seeds[10], (GENS, STATES), ((0, 256),), -0.2, 0.2), 0.0, 2.0),
    }


STEP_SIZE = 1.0


def rounded(values):
    return lax.optimization_barrier(values.astype(jnp.bfloat16)).astype(jnp.float32)


def one_generator(level_row, cost_row, state_total, successor, gen_prices):
    state_ids = jnp.arange(STATES, dtype=jnp.int32)
    valid_row = (state_ids < state_total).astype(jnp.float32)
    weights = valid_row[None, None, :] * jnp.exp(gen_prices[:, :, None] * level_row[None, None, :] - cost_row[None, None, :])
    weights = jnp.transpose(weights, (1, 0, 2))
    targets = successor.reshape(-1)
    branches = successor.shape[0]

    def push(state_now):
        spread_out = jnp.tile(rounded(state_now), (1, branches))
        return jnp.zeros_like(state_now).at[:, targets].add(spread_out)

    def pull(values):
        return jnp.sum(rounded(values)[:, successor], axis=1)

    opening = weights[0] / jnp.sum(weights[0], axis=-1, keepdims=True)

    def forward(state_now, present_weight):
        raised = push(state_now) * present_weight
        scale_now = jnp.sum(raised, axis=-1, keepdims=True)
        state_next = raised / scale_now
        return state_next, (state_next, scale_now)

    unused_state, (states_later, scales) = lax.scan(forward, opening, weights[1:])
    states_all = jnp.concatenate([opening[None], states_later], axis=0)

    def backward(back_now, inputs):
        present_weight, scale_now = inputs
        back_prev = pull(present_weight * back_now / scale_now)
        return back_prev, back_prev

    ones_back = jnp.ones_like(opening)
    unused_back, backs_earlier = lax.scan(backward, ones_back, (weights[1:], scales), reverse=True)
    backs_all = jnp.concatenate([backs_earlier, ones_back[None]], axis=0)
    combined_probability = states_all * backs_all
    output = jnp.sum(combined_probability * level_row[None, None, :], axis=-1) / jnp.sum(combined_probability, axis=-1)
    return jnp.transpose(output, (1, 0))


def reference(bus_price, bus_demand, multipliers, line_limits, ptdf_blocks, ptdf_pattern, gen_bus, state_counts, transitions, state_level, state_cost):
    gen_prices = jnp.transpose(jnp.take(bus_price, gen_bus, axis=2), (2, 0, 1))
    group_count = GENS // GEN_DEV
    members_all = (state_level, state_cost, state_counts, transitions, gen_prices)
    shaped = tuple(member.reshape((group_count, GEN_DEV) + member.shape[1:]) for member in members_all)

    def run_group(members):
        return jax.vmap(one_generator)(*members)

    generation = lax.map(run_group, shaped).reshape(GENS, SCN, HOURS)
    injections = jnp.zeros((SCN, HOURS, BUSES), jnp.float32).at[:, :, gen_bus].add(jnp.transpose(generation, (1, 2, 0)))
    net_blocks = rounded(injections - bus_demand).reshape(SCN, HOURS, BUSES // BLK, BLK)
    line_blocks = LINES // BLK

    def flow_block(members):
        block_ptdf, block_ids = members
        chosen = net_blocks[:, :, block_ids]
        return jnp.einsum('shkb,kbc->shc', chosen, block_ptdf.astype(jnp.float32))

    flows_all = lax.map(flow_block, (ptdf_blocks, ptdf_pattern))
    flows = jnp.transpose(flows_all, (1, 2, 0, 3)).reshape(SCN, HOURS, LINES)
    upper_old = multipliers[0]
    lower_old = multipliers[1]
    upper_new = jnp.maximum(0.0, upper_old + STEP_SIZE * (flows - line_limits[None, None, :]))
    lower_new = jnp.maximum(0.0, lower_old + STEP_SIZE * (-flows - line_limits[None, None, :]))
    change = rounded((upper_new - upper_old) - (lower_new - lower_old))
    change_blocks = jnp.transpose(change.reshape(SCN, HOURS, line_blocks, BLK), (2, 0, 1, 3))

    def add_block(accumulated, members):
        block_ptdf, block_ids, block_change = members
        spread = jnp.einsum('shc,kbc->shkb', block_change, block_ptdf.astype(jnp.float32))
        return accumulated.at[:, :, block_ids].add(spread), None

    initial = jnp.zeros((SCN, HOURS, BUSES // BLK, BLK), jnp.float32)
    price_change, unused_out = lax.scan(add_block, initial, (ptdf_blocks, ptdf_pattern, change_blocks))
    new_price = bus_price - price_change.reshape(SCN, HOURS, BUSES)
    return jnp.stack([upper_new, lower_new]), new_price
```

```python
import functools

import jax
import jax.numpy as jnp
from jax import lax
from jax.experimental import pallas as pl
from jax.experimental.pallas import tpu as pltpu
from jax.sharding import PartitionSpec as P

STATES = 512
SMALL = 256
BIG_DEV = 6
GEN_DEV = 16
BLK = 128
NNZB = 16
HOURS = 12
SCN = 32
SCN_DEV = 4
ROWS = SCN_DEV * HOURS
BUS_DEV = 512
NX, NZ, NGEN = 4, 8, 8
LINE_BLKS = 6
F32, BF16, I32 = jnp.float32, jnp.bfloat16, jnp.int32
MESH = pl.DeviceIdType.MESH
NN = (((1,), (0,)), ((), ()))
NT = (((1,), (1,)), ((), ()))
VMEM_LIMIT = 58 * 1024 * 1024


def dot(a, b, dims):
    return lax.dot_general(a, b, dims, preferred_element_type=F32)


def split3(value):
    high = value.astype(BF16)
    rest = value - high.astype(F32)
    middle = rest.astype(BF16)
    low = (rest - middle.astype(F32)).astype(BF16)
    return high, middle, low


def plan_kernel(
    counts,
    gen_bus,
    trans,
    level,
    cost,
    price,
    out,
    order,
    padded,
    prices,
    levels,
    costs,
    op_big,
    op_small,
    fwd,
    bwd,
    fwd_now,
    bwd_now,
    result,
):
    base = lax.axis_index("gen") * GEN_DEV

    def place(g, big_so_far):
        big = (counts[g] > SMALL).astype(I32)
        slot = jnp.where(big == 1, big_so_far, GEN_DEV - 1 - (g - big_so_far))
        order[slot] = g
        return big_so_far + big

    lax.fori_loop(0, GEN_DEV, place, jnp.int32(0))

    lane = lax.broadcasted_iota(I32, (1, BLK), 1)
    offset_row = jnp.full((1, BLK), -1, I32)
    own_offsets = jnp.zeros((1, BLK), F32)
    for slot in range(GEN_DEV):
        offset = lax.rem(gen_bus[order[slot]], BUS_DEV)
        offset_row = jnp.where(lane == slot, offset, offset_row)
        own_offsets = jnp.where(lane == base + slot, offset.astype(F32), own_offsets)

    padded[:, HOURS:, :] = jnp.zeros((SCN, 16 - HOURS, BUS_DEV), F32)
    padded[:, :HOURS, :] = price[...]
    onehot = (lax.broadcasted_iota(I32, (BUS_DEV, BLK), 0) == offset_row).astype(BF16)
    pieces = split3(padded[...].reshape(SCN * 16, BUS_DEV))
    prices[...] = dot(pieces[0], onehot, NN) + dot(pieces[1], onehot, NN) + dot(pieces[2], onehot, NN)

    state_ids = lax.broadcasted_iota(I32, (1, STATES), 1)
    for slot in range(GEN_DEV):
        g = order[slot]
        levels[slot : slot + 1, :] = level[pl.ds(g, 1), :]
        costs[slot : slot + 1, :] = jnp.where(state_ids < counts[g], cost[pl.ds(g, 1), :], 1e4)

    chunk = 64
    for slot in range(GEN_DEV):
        g = order[slot]
        span = STATES if slot < BIG_DEV else SMALL
        table = op_big.at[slot] if slot < BIG_DEV else op_small.at[slot - BIG_DEV]
        targets = [trans[g, j : j + 1, :span] for j in range(3)]

        def build(part, carry, targets=targets, span=span, table=table):
            start = pl.multiple_of(part * chunk, chunk)
            ids = lax.broadcasted_iota(I32, (chunk, span), 0) + start
            hits = [jnp.where(target == ids, 1.0, 0.0) for target in targets]
            table[pl.ds(start, chunk), :] = (hits[0] + hits[1] + hits[2]).astype(BF16)
            return carry

        lax.fori_loop(0, span // chunk, build, 0)

    def span_of(slot):
        return STATES if slot < BIG_DEV else SMALL

    def operator(slot):
        return op_big[slot] if slot < BIG_DEV else op_small[slot - BIG_DEV]

    def hour_price(hour):
        return prices[pl.ds(hour, SCN, stride=16), :]

    def weight(slot, price_now):
        span = span_of(slot)
        return jnp.exp(
            price_now[:, slot : slot + 1] * levels[slot : slot + 1, :span] - costs[slot : slot + 1, :span]
        )

    def unit(value):
        return value * (1.0 / jnp.sum(value, axis=1, keepdims=True))

    def step_forward(slot, price_now):
        raised = dot(fwd_now[slot, :, : span_of(slot)], operator(slot), NT) * weight(slot, price_now)
        state = unit(raised)
        fwd_now[slot, :, : span_of(slot)] = state.astype(BF16)
        return state

    def step_backward(slot, price_now):
        back = dot(bwd_now[slot, :, : span_of(slot)], operator(slot), NN)
        bwd_now[slot, :, : span_of(slot)] = unit(back * weight(slot, price_now)).astype(BF16)
        return back

    first, last = hour_price(0), hour_price(HOURS - 1)
    for slot in range(GEN_DEV):
        span = span_of(slot)
        state = unit(weight(slot, first))
        fwd[0, slot, :, :span] = state
        fwd_now[slot, :, :span] = state.astype(BF16)
        bwd[0, slot, :, :span] = jnp.ones((SCN, span), F32)
        bwd_now[slot, :, :span] = unit(weight(slot, last)).astype(BF16)

    def early(k, carry):
        price_f, price_b = hour_price(k), hour_price(HOURS - 1 - k)
        for slot in range(GEN_DEV):
            span = span_of(slot)
            fwd[k, slot, :, :span] = step_forward(slot, price_f)
            bwd[k, slot, :, :span] = step_backward(slot, price_b)
        return carry

    lanes = lax.broadcasted_iota(I32, (SCN, BLK), 1) - base

    def mean_level(slot, state, back):
        combined = state * back
        span = span_of(slot)
        top = jnp.sum(combined * levels[slot : slot + 1, :span], axis=1, keepdims=True)
        return top / jnp.sum(combined, axis=1, keepdims=True)

    def late(k, carry):
        other = HOURS - 1 - k
        price_f, price_b = hour_price(k), hour_price(other)
        at_k = jnp.zeros((SCN, BLK), F32)
        at_other = jnp.zeros((SCN, BLK), F32)
        for slot in range(GEN_DEV):
            span = span_of(slot)
            state = step_forward(slot, price_f)
            back = step_backward(slot, price_b)
            at_k = jnp.where(lanes == slot, mean_level(slot, state, bwd[other, slot, :, :span]), at_k)
            at_other = jnp.where(lanes == slot, mean_level(slot, fwd[other, slot, :, :span], back), at_other)
        result[k] = at_k
        result[other] = at_other
        return carry

    half = HOURS // 2
    lax.fori_loop(1, half, early, 0)
    lax.fori_loop(half, HOURS, late, 0)

    for t in range(HOURS):
        out[pl.ds(t, SCN, stride=16), :] = result[t]
    out[pl.ds(HOURS, SCN, stride=16), :] = jnp.broadcast_to(own_offsets, (SCN, BLK))
    for t in range(HOURS + 1, 16):
        out[pl.ds(t, SCN, stride=16), :] = jnp.zeros((SCN, BLK), F32)


def plan(counts, gen_bus, trans, level, cost, price):
    vmem = pl.BlockSpec(memory_space=pltpu.VMEM)
    smem = pl.BlockSpec(memory_space=pltpu.SMEM)
    half = HOURS // 2
    return pl.pallas_call(
        plan_kernel,
        name="plan",
        out_shape=jax.ShapeDtypeStruct((SCN * 16, BLK), F32),
        in_specs=[smem, smem, vmem, vmem, vmem, vmem],
        out_specs=vmem,
        scratch_shapes=[
            pltpu.SMEM((GEN_DEV,), I32),
            pltpu.VMEM((SCN, 16, BUS_DEV), F32),
            pltpu.VMEM((SCN * 16, BLK), F32),
            pltpu.VMEM((GEN_DEV, STATES), F32),
            pltpu.VMEM((GEN_DEV, STATES), F32),
            pltpu.VMEM((BIG_DEV, STATES, STATES), BF16),
            pltpu.VMEM((GEN_DEV - BIG_DEV, SMALL, SMALL), BF16),
            pltpu.VMEM((half, GEN_DEV, SCN, STATES), F32),
            pltpu.VMEM((half, GEN_DEV, SCN, STATES), F32),
            pltpu.VMEM((GEN_DEV, SCN, STATES), BF16),
            pltpu.VMEM((GEN_DEV, SCN, STATES), BF16),
            pltpu.VMEM((HOURS, SCN, BLK), F32),
        ],
        compiler_params=pltpu.CompilerParams(vmem_limit_bytes=VMEM_LIMIT),
    )(counts, gen_bus, trans, level, cost, price)


class Links:
    def __init__(self, send, recv):
        self.send, self.recv, self.used, self.copies = send, recv, 0, {}
        self.x = lax.div(lax.axis_index("bus"), NZ)
        self.z = lax.rem(lax.axis_index("bus"), NZ)
        self.g = lax.axis_index("gen")

    def xs(self, step):
        return lax.rem(self.x + step + NX, NX)

    def zs(self, step):
        return lax.rem(self.z + step + NZ, NZ)

    def gs(self, step):
        return lax.rem(self.g + step + NGEN, NGEN)

    def along_x(self, step):
        return {"bus": self.xs(step) * NZ + self.z}

    def along_z(self, step):
        return {"bus": self.x * NZ + self.zs(step)}

    def along_gen(self, step):
        return {"gen": self.gs(step)}

    def start(self, key, src, dst, target):
        index = self.used
        self.used += 1
        copy = pltpu.make_async_remote_copy(
            src_ref=src,
            dst_ref=dst,
            send_sem=self.send.at[index],
            recv_sem=self.recv.at[index],
            device_id=target,
            device_id_type=MESH,
        )
        copy.start()
        self.copies[key] = copy

    def arrived(self, key):
        self.copies[key].wait_recv()

    def drain(self):
        for copy in self.copies.values():
            copy.wait_send()


def greet(targets):
    barrier = pltpu.get_barrier_semaphore()
    for target in targets:
        pl.semaphore_signal(barrier, inc=1, device_id=target, device_id_type=MESH)
    pl.semaphore_wait(barrier, len(targets))


def take_turns(*routines):
    waiting = list(routines)
    while waiting:
        for routine in list(waiting):
            if next(routine, "over") == "over":
                waiting.remove(routine)


def gather_z_first(net, buf):
    def block(dx, dz):
        return buf.at[net.xs(dx), net.zs(dz)]

    stages = [[0]] + [[-k, k] if k < NZ // 2 else [-k] for k in range(1, NZ // 2 + 1)]
    turn = 0
    for k, arrivals in enumerate(stages):
        for dz in arrivals:
            if k:
                net.arrived(("Az", dz))
            if dz <= 0 and k < NZ // 2:
                net.start(("Az", dz - 1), block(0, dz), block(0, dz), net.along_z(1))
            if dz >= 0 and k < NZ // 2 - 1:
                net.start(("Az", dz + 1), block(0, dz), block(0, dz), net.along_z(-1))
            net.start(("Ax", -1, dz), block(0, dz), block(0, dz), net.along_x(1))
            net.start(("Ax", 1, dz), block(0, dz), block(0, dz), net.along_x(-1))
        if k:
            for dz in stages[k - 1]:
                turn = relay(net, block, dz, turn)
        yield
    for dz in stages[-1]:
        turn = relay(net, block, dz, turn)
    yield
    for arrivals in stages:
        for dz in arrivals:
            net.arrived(("Ax", 2, dz))


def relay(net, block, dz, turn):
    net.arrived(("Ax", -1, dz))
    if turn == 0:
        net.start(("Ax", 2, dz), block(-1, dz), block(-1, dz), net.along_x(1))
    net.arrived(("Ax", 1, dz))
    if turn == 1:
        net.start(("Ax", 2, dz), block(1, dz), block(1, dz), net.along_x(-1))
    return 1 - turn


def gather_x_first(net, buf):
    def block(dx, dz):
        return buf.at[net.xs(dx), net.zs(dz)]

    def ring_step(dx, k):
        if k:
            net.arrived(("Bz", dx, -k))
        if k < NZ // 2:
            net.start(("Bz", dx, -k - 1), block(dx, -k), block(dx, -k), net.along_z(1))
        if 0 < k < NZ // 2:
            net.arrived(("Bz", dx, k))
        if k < NZ // 2 - 1:
            net.start(("Bz", dx, k + 1), block(dx, k), block(dx, k), net.along_z(-1))

    net.start(("Bx", -1), block(0, 0), block(0, 0), net.along_x(1))
    net.start(("Bx", 1), block(0, 0), block(0, 0), net.along_x(-1))
    ring_step(0, 0)
    yield
    net.arrived(("Bx", -1))
    net.start(("Bx", 2, 0), block(-1, 0).at[0], block(-1, 0).at[0], net.along_x(1))
    net.arrived(("Bx", 1))
    net.start(("Bx", 2, 1), block(1, 0).at[1], block(1, 0).at[1], net.along_x(-1))
    ring_step(-1, 0)
    ring_step(1, 0)
    ring_step(0, 1)
    yield
    net.arrived(("Bx", 2, 0))
    net.arrived(("Bx", 2, 1))
    ring_step(2, 0)
    for stage in range(2, NZ // 2 + 3):
        for dx, begin in ((0, 0), (-1, 1), (1, 1), (2, 2)):
            if 0 < stage - begin <= NZ // 2:
                ring_step(dx, stage - begin)
        yield


GATHER_COPIES = 7 + 31 + 32


def gather_kernel(generation, demand, out, own, peers, netf, buf, send, recv, done):
    net = Links(send, recv)
    neighbours = [net.along_x(1), net.along_x(-1), net.along_z(1), net.along_z(-1)]
    greet([net.along_gen(i) for i in range(1, NGEN)] + neighbours)

    share = SCN_DEV * 16
    for i in range(1, NGEN):
        src = generation.at[pl.ds(pl.multiple_of(net.gs(i) * share, share), share), :]
        net.start(("gen", i), src, peers.at[i], net.along_gen(i))
    total = generation[pl.ds(pl.multiple_of(net.g * share, share), share), :]
    for i in range(1, NGEN):
        net.arrived(("gen", i))
        total = total + peers[i]

    offsets = total[HOURS : HOURS + 1, :]
    spots = lax.broadcasted_iota(I32, (BUS_DEV, BLK), 0).astype(F32)
    onehot = (spots == offsets).astype(BF16)
    high, middle, low = split3(total)
    injections = dot(high, onehot, NT) + dot(middle, onehot, NT) + dot(low, onehot, NT)
    for n in range(SCN_DEV):
        netf[n * HOURS : (n + 1) * HOURS, :] = injections[n * 16 : n * 16 + HOURS, :] - demand[n]
    rounded = netf[...].astype(BF16)
    for half in range(2):
        for c in range(2):
            column = (half * 2 + c) * BLK
            buf[half, net.x, net.z, c] = rounded[:, column : column + BLK]

    take_turns(gather_z_first(net, buf.at[0]), gather_x_first(net, buf.at[1]))
    net.drain()
    copy = pltpu.make_async_copy(buf, out, done)
    copy.start()
    copy.wait()


def gather(generation, demand):
    vmem = pl.BlockSpec(memory_space=pltpu.VMEM)
    shape = (2, NX, NZ, 2, ROWS, BLK)
    return pl.pallas_call(
        gather_kernel,
        name="gather",
        out_shape=jax.ShapeDtypeStruct(shape, BF16),
        in_specs=[vmem, vmem],
        out_specs=pl.BlockSpec(memory_space=pl.ANY),
        scratch_shapes=[
            pltpu.VMEM((8, 128), F32),
            pltpu.VMEM((NGEN, SCN_DEV * 16, BLK), F32),
            pltpu.VMEM((ROWS, BUS_DEV), F32),
            pltpu.VMEM(shape, BF16),
            pltpu.SemaphoreType.DMA((GATHER_COPIES,)),
            pltpu.SemaphoreType.DMA((GATHER_COPIES,)),
            pltpu.SemaphoreType.DMA,
        ],
        compiler_params=pltpu.CompilerParams(
            collective_id=0, has_side_effects=True, vmem_limit_bytes=VMEM_LIMIT
        ),
    )(generation, demand)


def place_of(block):
    device, c = lax.div(block, 4), lax.rem(block, 4)
    return (lax.div(c, 2) * (NX * NZ) + device) * 2 + lax.rem(c, 2)


def flow_kernel(pattern, nets, ptdf, mult, limits, new_mult, shares, total, changes):
    total[...] = jnp.zeros(total.shape, F32)
    for line in range(LINE_BLKS):
        lanes = slice(line * BLK, (line + 1) * BLK)
        places = [place_of(pattern[line, j]) for j in range(NNZB)]
        flow = jnp.zeros((ROWS, BLK), F32)
        for j in range(0, NNZB, 2):
            pair = jnp.concatenate([nets[places[j]], nets[places[j + 1]]], axis=1)
            flow = flow + dot(pair, ptdf[line, j : j + 2].reshape(2 * BLK, BLK), NN)
        limit = limits[:, lanes]
        for n in range(SCN_DEV):
            here = flow[n * HOURS : (n + 1) * HOURS, :]
            upper_old, lower_old = mult[0, n, :, lanes], mult[1, n, :, lanes]
            upper = jnp.maximum(0.0, upper_old + (here - limit))
            lower = jnp.maximum(0.0, lower_old + (-here - limit))
            new_mult[0, n, :, lanes] = upper
            new_mult[1, n, :, lanes] = lower
            changes[n * HOURS : (n + 1) * HOURS, :] = (upper - upper_old) - (lower - lower_old)
        change = changes[...].astype(BF16)
        spread = dot(change, ptdf[line].reshape(NNZB * BLK, BLK), NT)
        for j in range(NNZB):
            total[places[j]] += spread[:, j * BLK : (j + 1) * BLK]
    shares[...] = total[...].astype(BF16)


def flows(pattern, nets, ptdf, mult, limits):
    vmem = pl.BlockSpec(memory_space=pltpu.VMEM)
    smem = pl.BlockSpec(memory_space=pltpu.SMEM)
    return pl.pallas_call(
        flow_kernel,
        name="flows",
        out_shape=(
            jax.ShapeDtypeStruct(mult.shape, F32),
            jax.ShapeDtypeStruct(nets.shape, BF16),
        ),
        in_specs=[smem, vmem, vmem, vmem, vmem],
        out_specs=(vmem, vmem),
        scratch_shapes=[
            pltpu.VMEM(nets.shape, F32),
            pltpu.VMEM((ROWS, BLK), F32),
        ],
        compiler_params=pltpu.CompilerParams(vmem_limit_bytes=VMEM_LIMIT),
    )(pattern, nets, ptdf, mult, limits)


def wide(value):
    return value.astype(F32)


def reduce_z_first(net, part, right, left, out_right, out_left, kept, sent, arrived, final):
    deep = NZ // 2
    columns = range(NX)
    for dx in columns:
        net.start(("Ar", 1, dx), part.at[net.xs(dx), net.zs(deep)], right.at[0, dx], net.along_z(1))
        net.start(("Al", 1, dx), part.at[net.xs(dx), net.zs(1 - deep)], left.at[0, dx], net.along_z(-1))
    yield
    for k in range(1, deep):
        for dx in columns:
            net.arrived(("Ar", k, dx))
            mine = part[net.xs(dx), net.zs(deep - k)]
            out_right[k - 1, dx] = (wide(right[k - 1, dx]) + wide(mine)).astype(BF16)
            net.start(("Ar", k + 1, dx), out_right.at[k - 1, dx], right.at[k, dx], net.along_z(1))
            if k < deep - 1:
                net.arrived(("Al", k, dx))
                mine = part[net.xs(dx), net.zs(1 - deep + k)]
                out_left[k - 1, dx] = (wide(left[k - 1, dx]) + wide(mine)).astype(BF16)
                net.start(("Al", k + 1, dx), out_left.at[k - 1, dx], left.at[k, dx], net.along_z(-1))
        yield
    for dx in (1, 2, 3, 0):
        net.arrived(("Al", deep - 1, dx))
        net.arrived(("Ar", deep, dx))
        value = wide(part[net.xs(dx), net.z]) + wide(right[deep - 1, dx]) + wide(left[deep - 2, dx])
        if dx:
            sent[dx] = value.astype(BF16)
            net.start(("Ax", dx), sent.at[dx], arrived.at[dx], net.along_x(dx))
        else:
            kept[...] = value
    yield
    value = kept[...]
    for dx in (1, 3, 2):
        net.arrived(("Ax", dx))
        value = value + wide(arrived[dx])
    final[...] = value.astype(BF16)
    yield from spread_result(net, 0)


def reduce_x_first(net, part, first, second, out_second, kept, sent, arrived, final):
    half = NZ // 2
    low, high = pl.ds(0, half), pl.ds(half, half)
    net.start(("B1", 0), part.at[net.xs(2), low], first.at[0], net.along_x(1))
    net.start(("B1", 1), part.at[net.xs(2), high], first.at[1], net.along_x(-1))
    net.start(("B2", 0, 1), part.at[net.xs(1), high], second.at[0, high], net.along_x(1))
    net.start(("B2", 1, 0), part.at[net.xs(-1), low], second.at[1, low], net.along_x(-1))
    yield
    net.arrived(("B1", 0))
    out_second[0] = (wide(first[0]) + wide(part[net.xs(1), low])).astype(BF16)
    net.start(("B2", 0, 0), out_second.at[0], second.at[0, low], net.along_x(1))
    net.arrived(("B1", 1))
    out_second[1] = (wide(first[1]) + wide(part[net.xs(-1), high])).astype(BF16)
    net.start(("B2", 1, 1), out_second.at[1], second.at[1, high], net.along_x(-1))
    yield
    for key in ((0, 1), (1, 0), (0, 0), (1, 1)):
        net.arrived(("B2",) + key)
    for dz in (4, 3, 5, 2, 6, 1, 7, 0):
        z = net.zs(dz)
        value = wide(part[net.x, z]) + wide(second[0, z]) + wide(second[1, z])
        if dz:
            sent[dz] = value.astype(BF16)
            net.start(("Bz", dz), sent.at[dz], arrived.at[dz], net.along_z(dz))
        else:
            kept[...] = value
    yield
    yield
    value = kept[...]
    for dz in (1, 7, 2, 6, 3, 5, 4):
        net.arrived(("Bz", dz))
        value = value + wide(arrived[dz])
    final[...] = value.astype(BF16)
    yield from spread_result(net, 1)


def spread_result(net, half):
    for i in range(1, NGEN):
        net.start(("gen", half, i), net.finals.at[0, half], net.finals.at[i, half], net.along_gen(i))
    yield


REDUCE_COPIES = 4 * 7 + 3 + 6 + 7 + 14


def reduce_kernel(
    shares,
    price,
    out,
    a_right,
    a_left,
    a_out_right,
    a_out_left,
    a_kept,
    a_sent,
    a_arrived,
    b_first,
    b_second,
    b_out,
    b_kept,
    b_sent,
    b_arrived,
    finals,
    send,
    recv,
):
    net = Links(send, recv)
    net.finals = finals
    greet(
        [net.along_x(i) for i in range(1, NX)]
        + [net.along_z(i) for i in range(1, NZ)]
        + [net.along_gen(i) for i in range(1, NGEN)]
    )
    take_turns(
        reduce_z_first(
            net, shares.at[0], a_right, a_left, a_out_right, a_out_left, a_kept, a_sent, a_arrived, finals.at[0, 0]
        ),
        reduce_x_first(net, shares.at[1], b_first, b_second, b_out, b_kept, b_sent, b_arrived, finals.at[0, 1]),
    )
    for i in range(NGEN):
        first = net.gs(-i) * SCN_DEV
        for half in range(2):
            if i:
                net.arrived(("gen", half, i))
            for c in range(2):
                columns = slice((half * 2 + c) * BLK, (half * 2 + c + 1) * BLK)
                change = wide(finals[i, half, c])
                for n in range(SCN_DEV):
                    out[first + n, :, columns] = (
                        price[first + n, :, columns] - change[n * HOURS : (n + 1) * HOURS, :]
                    )
    net.drain()


def reduce(shares, price):
    vmem = pl.BlockSpec(memory_space=pltpu.VMEM)
    piece = (2, ROWS, BLK)
    deep = NZ // 2
    return pl.pallas_call(
        reduce_kernel,
        name="reduce",
        out_shape=jax.ShapeDtypeStruct(price.shape, F32),
        in_specs=[vmem, vmem],
        out_specs=vmem,
        scratch_shapes=[
            pltpu.VMEM((deep, NX) + piece, BF16),
            pltpu.VMEM((deep - 1, NX) + piece, BF16),
            pltpu.VMEM((deep - 1, NX) + piece, BF16),
            pltpu.VMEM((deep - 2, NX) + piece, BF16),
            pltpu.VMEM(piece, F32),
            pltpu.VMEM((NX,) + piece, BF16),
            pltpu.VMEM((NX,) + piece, BF16),
            pltpu.VMEM((2, NZ // 2) + piece, BF16),
            pltpu.VMEM((2, NZ) + piece, BF16),
            pltpu.VMEM((2, NZ // 2) + piece, BF16),
            pltpu.VMEM(piece, F32),
            pltpu.VMEM((NZ,) + piece, BF16),
            pltpu.VMEM((NZ,) + piece, BF16),
            pltpu.VMEM((NGEN, 2) + piece, BF16),
            pltpu.SemaphoreType.DMA((REDUCE_COPIES,)),
            pltpu.SemaphoreType.DMA((REDUCE_COPIES,)),
        ],
        compiler_params=pltpu.CompilerParams(
            collective_id=1, has_side_effects=True, vmem_limit_bytes=VMEM_LIMIT
        ),
    )(shares, price)


def shards(
    bus_price,
    bus_demand,
    multipliers,
    line_limits,
    ptdf_blocks,
    ptdf_pattern,
    gen_bus,
    state_counts,
    transitions,
    state_level,
    state_cost,
):
    generation = plan(state_counts, gen_bus, transitions, state_level, state_cost, bus_price)
    nets = gather(generation, bus_demand)
    flat = (2 * NX * NZ * 2, ROWS, BLK)
    new_mult, shares = flows(
        ptdf_pattern, nets.reshape(flat), ptdf_blocks, multipliers, line_limits.reshape(1, -1)
    )
    new_price = reduce(shares.reshape(nets.shape), bus_price)
    return new_mult, new_price


def solution(mesh):
    in_specs = (
        P(None, None, "bus"),
        P("gen", None, "bus"),
        P(None, "gen", None, "bus"),
        P("bus"),
        P("bus", None, None, None),
        P("bus", None),
        P(("gen", "bus")),
        P(("gen", "bus")),
        P(("gen", "bus"), None, None),
        P(("gen", "bus"), None),
        P(("gen", "bus"), None),
    )
    out_specs = (P(None, "gen", None, "bus"), P(None, None, "bus"))
    return jax.shard_map(shards, mesh=mesh, in_specs=in_specs, out_specs=out_specs, check_vma=False)
```

```python
import functools

import jax
import jax.numpy as jnp
from jax import lax
from jax.experimental import pallas as pl
from jax.experimental.pallas import tpu as pltpu
from jax.sharding import PartitionSpec as P

STATES = 512
SMALL = 256
BIG_DEV = 6
GEN_DEV = 16
BLK = 128
NNZB = 16
HOURS = 12
SCN = 32
SCN_DEV = 4
ROWS = SCN_DEV * HOURS
BUS_DEV = 512
NX, NZ, NGEN = 4, 8, 8
LINE_BLKS = 6
F32, BF16, I32 = jnp.float32, jnp.bfloat16, jnp.int32
MESH = pl.DeviceIdType.MESH
NN = (((1,), (0,)), ((), ()))
NT = (((1,), (1,)), ((), ()))
OFFSET_LANE = (HOURS % 8) * GEN_DEV
VMEM_LIMIT = 58 * 1024 * 1024


def dot(a, b, dims):
    return lax.dot_general(a, b, dims, preferred_element_type=F32)


def split3(value):
    high = value.astype(BF16)
    rest = value - high.astype(F32)
    middle = rest.astype(BF16)
    low = (rest - middle.astype(F32)).astype(BF16)
    return high, middle, low


def plan_kernel(
    counts,
    gen_bus,
    pattern,
    trans,
    level,
    cost,
    price,
    out,
    inverse,
    order,
    prices,
    levels,
    costs,
    op_big,
    op_small,
    fwd,
    bwd,
    fwd_now,
    bwd_now,
    result,
):
    def place(g, big_so_far):
        big = (counts[g] > SMALL).astype(I32)
        slot = jnp.where(big == 1, big_so_far, GEN_DEV - 1 - (g - big_so_far))
        order[slot] = g
        return big_so_far + big

    lax.fori_loop(0, GEN_DEV, place, jnp.int32(0))

    def clear(block, carry):
        for line in range(LINE_BLKS):
            inverse[line, block] = LINE_BLKS * NNZB
        return carry

    def invert(j, carry):
        for line in range(LINE_BLKS):
            inverse[line, pattern[line, j]] = line * NNZB + j
        return carry

    lax.fori_loop(0, NX * NZ * 4, clear, 0)
    lax.fori_loop(0, NNZB, invert, 0)

    lane = lax.broadcasted_iota(I32, (1, BLK), 1)
    offset_row = jnp.full((1, BLK), -1, I32)
    sent_offsets = jnp.zeros((1, BLK), F32)
    for slot in range(GEN_DEV):
        offset = lax.rem(gen_bus[order[slot]], BUS_DEV)
        offset_row = jnp.where(lane == slot, offset, offset_row)
        sent_offsets = jnp.where(lane == OFFSET_LANE + slot, offset.astype(F32), sent_offsets)

    onehot = (lax.broadcasted_iota(I32, (BUS_DEV, BLK), 0) == offset_row).astype(BF16)
    pieces = split3(price[...].reshape(HOURS * SCN, BUS_DEV))
    prices[...] = dot(pieces[0], onehot, NN) + dot(pieces[1], onehot, NN) + dot(pieces[2], onehot, NN)

    state_ids = lax.broadcasted_iota(I32, (1, STATES), 1)
    for slot in range(GEN_DEV):
        g = order[slot]
        levels[slot : slot + 1, :] = level[pl.ds(g, 1), :]
        costs[slot : slot + 1, :] = jnp.where(state_ids < counts[g], cost[pl.ds(g, 1), :], 1e4)

    chunk = 64
    for slot in range(GEN_DEV):
        g = order[slot]
        span = STATES if slot < BIG_DEV else SMALL
        table = op_big.at[slot] if slot < BIG_DEV else op_small.at[slot - BIG_DEV]
        targets = [trans[j, pl.ds(g, 1), :span] for j in range(3)]

        def build(part, carry, targets=targets, span=span, table=table):
            start = pl.multiple_of(part * chunk, chunk)
            ids = lax.broadcasted_iota(I32, (chunk, span), 0) + start
            hits = [jnp.where(target == ids, 1.0, 0.0) for target in targets]
            table[pl.ds(start, chunk), :] = (hits[0] + hits[1] + hits[2]).astype(BF16)
            return carry

        lax.fori_loop(0, span // chunk, build, 0)

    def span_of(slot):
        return STATES if slot < BIG_DEV else SMALL

    def operator(slot):
        return op_big[slot] if slot < BIG_DEV else op_small[slot - BIG_DEV]

    def hour_price(hour):
        return prices[pl.ds(pl.multiple_of(hour * SCN, SCN), SCN), :]

    def weight(slot, price_now):
        span = span_of(slot)
        return jnp.exp(
            price_now[:, slot : slot + 1] * levels[slot : slot + 1, :span] - costs[slot : slot + 1, :span]
        )

    def unit(value):
        return value * (1.0 / jnp.sum(value, axis=1, keepdims=True))

    def step_forward(slot, price_now):
        raised = dot(fwd_now[slot, :, : span_of(slot)], operator(slot), NT) * weight(slot, price_now)
        state = unit(raised)
        fwd_now[slot, :, : span_of(slot)] = state.astype(BF16)
        return state

    def step_backward(slot, price_now):
        back = dot(bwd_now[slot, :, : span_of(slot)], operator(slot), NN)
        bwd_now[slot, :, : span_of(slot)] = unit(back * weight(slot, price_now)).astype(BF16)
        return back

    first, last = hour_price(0), hour_price(HOURS - 1)
    for slot in range(GEN_DEV):
        span = span_of(slot)
        state = unit(weight(slot, first))
        fwd[0, slot, :, :span] = state
        fwd_now[slot, :, :span] = state.astype(BF16)
        bwd[0, slot, :, :span] = jnp.ones((SCN, span), F32)
        bwd_now[slot, :, :span] = unit(weight(slot, last)).astype(BF16)

    def early(k, carry):
        price_f, price_b = hour_price(k), hour_price(HOURS - 1 - k)
        for slot in range(GEN_DEV):
            span = span_of(slot)
            fwd[k, slot, :, :span] = step_forward(slot, price_f)
            bwd[k, slot, :, :span] = step_backward(slot, price_b)
        return carry

    lanes = lax.broadcasted_iota(I32, (SCN, BLK), 1)

    def mean_level(slot, state, back):
        combined = state * back
        span = span_of(slot)
        top = jnp.sum(combined * levels[slot : slot + 1, :span], axis=1, keepdims=True)
        return top / jnp.sum(combined, axis=1, keepdims=True)

    result[0] = jnp.zeros((SCN, BLK), F32)
    result[1] = jnp.broadcast_to(sent_offsets, (SCN, BLK))

    def late(k, carry):
        other = HOURS - 1 - k
        price_f, price_b = hour_price(k), hour_price(other)
        at_k = jnp.zeros((SCN, BLK), F32)
        at_other = jnp.zeros((SCN, BLK), F32)
        lanes_k = lanes - lax.rem(k, 8) * GEN_DEV
        lanes_other = lanes - other * GEN_DEV
        for slot in range(GEN_DEV):
            span = span_of(slot)
            state = step_forward(slot, price_f)
            back = step_backward(slot, price_b)
            at_k = jnp.where(lanes_k == slot, mean_level(slot, state, bwd[other, slot, :, :span]), at_k)
            at_other = jnp.where(lanes_other == slot, mean_level(slot, fwd[other, slot, :, :span], back), at_other)
        result[lax.div(k, 8)] += at_k
        result[0] += at_other
        return carry

    half = HOURS // 2
    lax.fori_loop(1, half, early, 0)
    lax.fori_loop(half, HOURS, late, 0)

    for owner in range(NGEN):
        rows = slice(owner * SCN_DEV, (owner + 1) * SCN_DEV)
        for part in range(2):
            out[owner, part * SCN_DEV : (part + 1) * SCN_DEV, :] = result[part, rows, :]


def plan(counts, gen_bus, pattern, trans, level, cost, price):
    vmem = pl.BlockSpec(memory_space=pltpu.VMEM)
    smem = pl.BlockSpec(memory_space=pltpu.SMEM)
    half = HOURS // 2
    return pl.pallas_call(
        plan_kernel,
        name="plan",
        out_shape=(
            jax.ShapeDtypeStruct((NGEN, 2 * SCN_DEV, BLK), F32),
            jax.ShapeDtypeStruct((LINE_BLKS, NX * NZ * 4), I32),
        ),
        in_specs=[smem, smem, smem, vmem, vmem, vmem, vmem],
        out_specs=(vmem, smem),
        scratch_shapes=[
            pltpu.SMEM((GEN_DEV,), I32),
            pltpu.VMEM((HOURS * SCN, BLK), F32),
            pltpu.VMEM((GEN_DEV, STATES), F32),
            pltpu.VMEM((GEN_DEV, STATES), F32),
            pltpu.VMEM((BIG_DEV, STATES, STATES), BF16),
            pltpu.VMEM((GEN_DEV - BIG_DEV, SMALL, SMALL), BF16),
            pltpu.VMEM((half, GEN_DEV, SCN, STATES), F32),
            pltpu.VMEM((half, GEN_DEV, SCN, STATES), F32),
            pltpu.VMEM((GEN_DEV, SCN, STATES), BF16),
            pltpu.VMEM((GEN_DEV, SCN, STATES), BF16),
            pltpu.VMEM((2, SCN, BLK), F32),
        ],
        compiler_params=pltpu.CompilerParams(vmem_limit_bytes=VMEM_LIMIT),
    )(counts, gen_bus, pattern, trans, level, cost, price)


class Links:
    def __init__(self, send, recv):
        self.send, self.recv, self.used, self.copies = send, recv, 0, {}
        self.x = lax.div(lax.axis_index("bus"), NZ)
        self.z = lax.rem(lax.axis_index("bus"), NZ)
        self.g = lax.axis_index("gen")

    def xs(self, step):
        return lax.rem(self.x + step + NX, NX)

    def zs(self, step):
        return lax.rem(self.z + step + NZ, NZ)

    def gs(self, step):
        return lax.rem(self.g + step + NGEN, NGEN)

    def along_x(self, step):
        return {"bus": self.xs(step) * NZ + self.z}

    def along_z(self, step):
        return {"bus": self.x * NZ + self.zs(step)}

    def along_gen(self, step):
        return {"gen": self.gs(step)}

    def start(self, key, src, dst, target):
        index = self.used
        self.used += 1
        copy = pltpu.make_async_remote_copy(
            src_ref=src,
            dst_ref=dst,
            send_sem=self.send.at[index],
            recv_sem=self.recv.at[index],
            device_id=target,
            device_id_type=MESH,
        )
        copy.start()
        assert key not in self.copies
        self.copies[key] = copy

    def arrived(self, key):
        self.copies[key].wait_recv()

    def drain(self):
        for copy in self.copies.values():
            copy.wait_send()


def greet(targets):
    barrier = pltpu.get_barrier_semaphore()
    for target in targets:
        pl.semaphore_signal(barrier, inc=1, device_id=target, device_id_type=MESH)
    pl.semaphore_wait(barrier, len(targets))


def take_turns(*routines):
    waiting = list(routines)
    while waiting:
        for routine in list(waiting):
            if next(routine, "over") == "over":
                waiting.remove(routine)


def gather_z_first(net, buf):
    def block(dx, dz):
        return buf.at[net.xs(dx), net.zs(dz)]

    def pass_on(dz):
        for i in (1, -1, 2):
            net.start(("Ax", i, dz), block(0, dz), block(0, dz), net.along_x(i))

    for dz in (4, 3, -3, 2, -2, 1, -1):
        net.start(("Az", dz), block(0, 0), block(0, 0), net.along_z(dz))
    pass_on(0)
    yield
    for group in ((1, -1), (2, -2), (3, -3), (4,)):
        for dz in group:
            net.arrived(("Az", dz))
            pass_on(-dz)
        yield
    for dz in (0, -1, 1, -2, 2, -3, 3, -4):
        for i in (1, -1, 2):
            net.arrived(("Ax", i, dz))


def gather_x_first(net, buf):
    def block(dx, dz):
        return buf.at[net.xs(dx), net.zs(dz)]

    def first(dx):
        for i in (2, -2, 1, -1):
            net.start(("Bz", dx, i), block(dx, 0), block(dx, 0), net.along_z(i))

    def second(dx):
        for i in (2, -2):
            near = i // 2
            c = 0 if i > 0 else 1
            net.arrived(("Bz", dx, i))
            net.start(("Bz4", dx, i), block(dx, -i).at[c], block(dx, -i).at[c], net.along_z(i))
            net.start(("Bz3", dx, i), block(dx, -i), block(dx, -i), net.along_z(near))

    for i in (2, 1, -1):
        net.start(("Bx", i), block(0, 0), block(0, 0), net.along_x(i))
    first(0)
    yield
    for i in (-1, 1, 2):
        net.arrived(("Bx", i))
        first(-i)
    yield
    second(0)
    yield
    second(1)
    second(-1)
    yield
    second(-2)
    yield
    for dx in (0, 1, -1, -2):
        for i in (1, -1):
            net.arrived(("Bz", dx, i))
        for i in (2, -2):
            net.arrived(("Bz3", dx, i))
            net.arrived(("Bz4", dx, i))


def wide(value):
    return value.astype(F32)


def reduce_x_first(net, part, along_x, to_z, arrived, kept, final):
    far_first = (4, 3, 5, 2, 6, 1, 7, 0)
    for dz in far_first:
        for n, i in enumerate((2, 1, -1)):
            net.start(("sum Ax", n, dz), part.at[net.xs(i), net.zs(dz)], along_x.at[n, dz], net.along_x(i))
    yield
    yield
    for dz in far_first:
        value = wide(part[net.x, net.zs(dz)])
        for n in range(3):
            net.arrived(("sum Ax", n, dz))
            value = value + wide(along_x[n, dz])
        if dz:
            to_z[dz] = value.astype(BF16)
            net.start(("sum Az", dz), to_z.at[dz], arrived.at[dz], net.along_z(dz))
        else:
            kept[...] = value
        if dz in (5, 6):
            yield
    yield
    value = kept[...]
    for dz in (1, 7, 2, 6, 3, 5, 4):
        net.arrived(("sum Az", dz))
        value = value + wide(arrived[dz])
    final[...] = value.astype(BF16)
    yield from spread_result(net, 0)


def reduce_z_first(net, part, near, third, fourth, to_two, from_two, to_x, arrived, kept, final):
    columns = (2, 1, 3, 0)
    for dx in columns:
        column = net.xs(dx)
        for n, i in enumerate((1, -1)):
            net.start(("sum B4", dx, n), part.at[column, net.zs(4), n], fourth.at[dx, n], net.along_z(2 * i))
            net.start(("sum B3", dx, n), part.at[column, net.zs(3 * i)], third.at[dx, n], net.along_z(i))
    for dx in columns:
        for n, i in enumerate((1, -1)):
            net.start(("sum B1", dx, n), part.at[net.xs(dx), net.zs(i)], near.at[dx, n], net.along_z(i))
    yield
    for dx in columns:
        for n, i in enumerate((1, -1)):
            net.arrived(("sum B3", dx, n))
            net.arrived(("sum B4", dx, n))
            value = wide(part[net.xs(dx), net.zs(2 * i)]) + wide(third[dx, n])
            to_two[dx, n, 1 - n] = value[1 - n].astype(BF16)
            to_two[dx, n, n] = (value[n] + wide(fourth[dx, n])).astype(BF16)
            net.start(("sum B2", dx, n), to_two.at[dx, n], from_two.at[dx, n], net.along_z(2 * i))
        if dx in (2, 3):
            yield
    yield
    for dx in columns:
        value = wide(part[net.xs(dx), net.z])
        for n in range(2):
            net.arrived(("sum B1", dx, n))
            net.arrived(("sum B2", dx, n))
            value = value + (wide(near[dx, n]) + wide(from_two[dx, n]))
        if dx:
            to_x[dx] = value.astype(BF16)
            net.start(("sum Bx", dx), to_x.at[dx], arrived.at[dx], net.along_x(dx))
        else:
            kept[...] = value
    yield
    value = kept[...]
    for dx in (1, 3, 2):
        net.arrived(("sum Bx", dx))
        value = value + wide(arrived[dx])
    final[...] = value.astype(BF16)
    yield from spread_result(net, 1)


def spread_result(net, half):
    for i in range(1, NGEN):
        mine = net.finals.at[net.g, half]
        net.start(("out", half, i), mine, mine, net.along_gen(i))
    yield


NET_COPIES = 7 + 31 + 35 + 31 + 35 + 14


def place_of(block):
    device, c = lax.div(block, 4), lax.rem(block, 4)
    return (lax.div(c, 2) * (NX * NZ) + device) * 2 + lax.rem(c, 2)


def network_kernel(
    pattern,
    inverse,
    generation,
    demand,
    mult,
    limits,
    ptdf_far,
    price_far,
    new_price,
    new_mult,
    peers,
    netf,
    nets,
    ptdf,
    price,
    changes,
    spreads,
    shares,
    a_x,
    a_to_z,
    a_arrived,
    a_kept,
    b_near,
    b_third,
    b_fourth,
    b_to_two,
    b_from_two,
    b_to_x,
    b_arrived,
    b_kept,
    finals,
    send,
    recv,
    done,
):
    net = Links(send, recv)
    net.finals = finals
    load_ptdf = pltpu.make_async_copy(ptdf_far, ptdf, done.at[0])
    load_price = pltpu.make_async_copy(price_far, price, done.at[1])
    load_ptdf.start()
    load_price.start()
    greet(
        [net.along_x(i) for i in range(1, NX)]
        + [net.along_z(i) for i in range(1, NZ)]
        + [net.along_gen(i) for i in range(1, NGEN)]
    )

    for i in range(1, NGEN):
        net.start(("gen", i), generation.at[net.gs(i)], peers.at[net.g], net.along_gen(i))
    peers[net.g] = generation[net.g]
    for i in range(1, NGEN):
        net.arrived(("gen", i))
    lane_group = lax.div(lax.broadcasted_iota(I32, (2 * SCN_DEV, BLK), 1), GEN_DEV)
    by_hour = [jnp.zeros((2 * SCN_DEV, BLK), F32) for hour in range(8)]
    for source in range(NGEN):
        packed = peers[source]
        for hour in range(8):
            moved = pltpu.roll(packed, (source - hour) % NGEN * GEN_DEV, 1) if source != hour else packed
            by_hour[hour] = jnp.where(lane_group == source, moved, by_hour[hour])
    hours = [by_hour[t % 8][t // 8 * SCN_DEV : (t // 8 + 1) * SCN_DEV, :] for t in range(HOURS)]
    offsets = by_hour[HOURS % 8][SCN_DEV : SCN_DEV + 1, :]
    total = jnp.concatenate(hours, axis=0)

    spots = wide(lax.broadcasted_iota(I32, (BUS_DEV, BLK), 0))
    onehot = (spots == offsets).astype(BF16)
    high, middle, low = split3(total)
    netf[...] = dot(high, onehot, NT) + dot(middle, onehot, NT) + dot(low, onehot, NT)
    for t in range(HOURS):
        netf[t * SCN_DEV : (t + 1) * SCN_DEV, :] -= demand[t]
    rounded = netf[...].astype(BF16)
    for half in range(2):
        for c in range(2):
            column = (half * 2 + c) * BLK
            nets[half, net.x, net.z, c] = rounded[:, column : column + BLK]

    take_turns(gather_z_first(net, nets.at[0]), gather_x_first(net, nets.at[1]))

    load_ptdf.wait()
    blocks = nets.reshape(2 * NX * NZ * 2, ROWS, BLK)
    spreads[LINE_BLKS * NNZB] = jnp.zeros((ROWS, BLK), F32)
    for line in range(LINE_BLKS):
        lanes = slice(line * BLK, (line + 1) * BLK)
        places = [place_of(pattern[line, j]) for j in range(NNZB)]
        flow = jnp.zeros((ROWS, BLK), F32)
        for j in range(0, NNZB, 2):
            pair = jnp.concatenate([blocks[places[j]], blocks[places[j + 1]]], axis=1)
            flow = flow + dot(pair, ptdf[line, j : j + 2].reshape(2 * BLK, BLK), NN)
        limit = limits[:, lanes]
        for t in range(HOURS):
            rows = slice(t * SCN_DEV, (t + 1) * SCN_DEV)
            here = flow[rows, :]
            upper_old, lower_old = mult[0, t, :, lanes], mult[1, t, :, lanes]
            upper = jnp.maximum(0.0, upper_old + (here - limit))
            lower = jnp.maximum(0.0, lower_old + (-here - limit))
            new_mult[0, t, :, lanes] = upper
            new_mult[1, t, :, lanes] = lower
            changes[rows, :] = (upper - upper_old) - (lower - lower_old)
        change = changes[...].astype(BF16)
        spread = dot(change, ptdf[line].reshape(NNZB * BLK, BLK), NT)
        for j in range(NNZB):
            spreads[line * NNZB + j] = spread[:, j * BLK : (j + 1) * BLK]

    def collect(device, carry):
        x, z = lax.div(device, NZ), lax.rem(device, NZ)
        for half in range(2):
            for c in range(2):
                block = device * 4 + half * 2 + c
                value = spreads[inverse[0, block]]
                for line in range(1, LINE_BLKS):
                    value = value + spreads[inverse[line, block]]
                shares[half, x, z, c] = value.astype(BF16)
        return carry

    lax.fori_loop(0, NX * NZ, collect, 0)

    take_turns(
        reduce_x_first(net, shares.at[0], a_x, a_to_z, a_arrived, a_kept, finals.at[net.g, 0]),
        reduce_z_first(
            net,
            shares.at[1],
            b_near,
            b_third,
            b_fourth,
            b_to_two,
            b_from_two,
            b_to_x,
            b_arrived,
            b_kept,
            finals.at[net.g, 1],
        ),
    )
    load_price.wait()
    for half in range(2):
        for i in range(1, NGEN):
            net.arrived(("out", half, i))
        for owner in range(NGEN):
            scenarios = slice(owner * SCN_DEV, (owner + 1) * SCN_DEV)
            for c in range(2):
                columns = slice((half * 2 + c) * BLK, (half * 2 + c + 1) * BLK)
                change = wide(finals[owner, half, c])
                for t in range(HOURS):
                    new_price[t, scenarios, columns] = (
                        price[t, scenarios, columns] - change[t * SCN_DEV : (t + 1) * SCN_DEV, :]
                    )
    net.drain()


def network(pattern, inverse, generation, demand, mult, limits, ptdf, price):
    vmem = pl.BlockSpec(memory_space=pltpu.VMEM)
    smem = pl.BlockSpec(memory_space=pltpu.SMEM)
    far = pl.BlockSpec(memory_space=pl.ANY)
    piece = (2, ROWS, BLK)
    everything = (2, NX, NZ) + piece
    return pl.pallas_call(
        network_kernel,
        name="network",
        out_shape=(
            jax.ShapeDtypeStruct(price.shape, F32),
            jax.ShapeDtypeStruct(mult.shape, F32),
        ),
        in_specs=[smem, smem, vmem, vmem, vmem, vmem, far, far],
        out_specs=(vmem, vmem),
        scratch_shapes=[
            pltpu.VMEM(generation.shape, F32),
            pltpu.VMEM((ROWS, BUS_DEV), F32),
            pltpu.VMEM(everything, BF16),
            pltpu.VMEM(ptdf.shape, BF16),
            pltpu.VMEM(price.shape, F32),
            pltpu.VMEM((ROWS, BLK), F32),
            pltpu.VMEM((LINE_BLKS * NNZB + 1, ROWS, BLK), F32),
            pltpu.VMEM(everything, BF16),
            pltpu.VMEM((3, NZ) + piece, BF16),
            pltpu.VMEM((NZ,) + piece, BF16),
            pltpu.VMEM((NZ,) + piece, BF16),
            pltpu.VMEM(piece, F32),
            pltpu.VMEM((NX, 2) + piece, BF16),
            pltpu.VMEM((NX, 2) + piece, BF16),
            pltpu.VMEM((NX, 2, ROWS, BLK), BF16),
            pltpu.VMEM((NX, 2) + piece, BF16),
            pltpu.VMEM((NX, 2) + piece, BF16),
            pltpu.VMEM((NX,) + piece, BF16),
            pltpu.VMEM((NX,) + piece, BF16),
            pltpu.VMEM(piece, F32),
            pltpu.VMEM((NGEN, 2) + piece, BF16),
            pltpu.SemaphoreType.DMA((NET_COPIES,)),
            pltpu.SemaphoreType.DMA((NET_COPIES,)),
            pltpu.SemaphoreType.DMA((2,)),
        ],
        compiler_params=pltpu.CompilerParams(
            collective_id=0, has_side_effects=True, vmem_limit_bytes=VMEM_LIMIT
        ),
    )(pattern, inverse, generation, demand, mult, limits, ptdf, price)


def shards(
    bus_price,
    bus_demand,
    multipliers,
    line_limits,
    ptdf_blocks,
    ptdf_pattern,
    gen_bus,
    state_counts,
    transitions,
    state_level,
    state_cost,
):
    price = bus_price.transpose(1, 0, 2)
    generation, inverse = plan(
        state_counts, gen_bus, ptdf_pattern, transitions.transpose(1, 0, 2), state_level, state_cost, price
    )
    new_price, new_mult = network(
        ptdf_pattern,
        inverse,
        generation,
        bus_demand.transpose(1, 0, 2),
        multipliers.transpose(0, 2, 1, 3),
        line_limits.reshape(1, -1),
        ptdf_blocks,
        price,
    )
    return new_mult.transpose(0, 2, 1, 3), new_price.transpose(1, 0, 2)


def solution(mesh):
    in_specs = (
        P(None, None, "bus"),
        P("gen", None, "bus"),
        P(None, "gen", None, "bus"),
        P("bus"),
        P("bus", None, None, None),
        P("bus", None),
        P(("gen", "bus")),
        P(("gen", "bus")),
        P(("gen", "bus"), None, None),
        P(("gen", "bus"), None),
        P(("gen", "bus"), None),
    )
    out_specs = (P(None, "gen", None, "bus"), P(None, None, "bus"))
    return jax.shard_map(shards, mesh=mesh, in_specs=in_specs, out_specs=out_specs, check_vma=False)
```

```python
import functools

import jax
import jax.numpy as jnp
from jax import lax
from jax.experimental import pallas as pl
from jax.experimental.pallas import tpu as pltpu
from jax.sharding import PartitionSpec as P

STATES = 512
SMALL = 256
BIG_DEV = 6
GEN_DEV = 16
BLK = 128
NNZB = 16
HOURS = 12
SCN = 32
SCN_DEV = 4
ROWS = SCN_DEV * HOURS
BUS_DEV = 512
NX, NZ, NGEN = 4, 8, 8
LINE_BLKS = 6
F32, BF16, I32 = jnp.float32, jnp.bfloat16, jnp.int32
MESH = pl.DeviceIdType.MESH
NN = (((1,), (0,)), ((), ()))
NT = (((1,), (1,)), ((), ()))
OFFSET_LANE = (HOURS % 8) * GEN_DEV
VMEM_LIMIT = 58 * 1024 * 1024


def dot(a, b, dims):
    return lax.dot_general(a, b, dims, preferred_element_type=F32)


def split3(value):
    high = value.astype(BF16)
    rest = value - high.astype(F32)
    middle = rest.astype(BF16)
    low = (rest - middle.astype(F32)).astype(BF16)
    return high, middle, low


def plan_kernel(
    counts,
    gen_bus,
    pattern,
    trans,
    level,
    cost,
    price,
    out,
    inverse,
    order,
    prices,
    levels,
    costs,
    op_big,
    op_small,
    turned_big,
    turned_small,
    fwd,
    bwd,
    fwd_now,
    bwd_now,
    result,
):
    def place(g, big_so_far):
        big = (counts[g] > SMALL).astype(I32)
        slot = jnp.where(big == 1, big_so_far, GEN_DEV - 1 - (g - big_so_far))
        order[slot] = g
        return big_so_far + big

    lax.fori_loop(0, GEN_DEV, place, jnp.int32(0))

    def clear(line):
        for block in range(NX * NZ * 4):
            inverse[line, block] = LINE_BLKS * NNZB

    def invert(line):
        for j in range(NNZB):
            inverse[line, pattern[line, j]] = line * NNZB + j

    clear(0)

    lane = lax.broadcasted_iota(I32, (1, BLK), 1)
    offset_row = jnp.full((1, BLK), -1, I32)
    sent_offsets = jnp.zeros((1, BLK), F32)
    for slot in range(GEN_DEV):
        offset = lax.rem(gen_bus[order[slot]], BUS_DEV)
        offset_row = jnp.where(lane == slot, offset, offset_row)
        sent_offsets = jnp.where(lane == OFFSET_LANE + slot, offset.astype(F32), sent_offsets)

    onehot = (lax.broadcasted_iota(I32, (BUS_DEV, BLK), 0) == offset_row).astype(BF16)
    pieces = split3(price[...].reshape(HOURS * SCN, BUS_DEV))
    prices[...] = dot(pieces[0], onehot, NN) + dot(pieces[1], onehot, NN) + dot(pieces[2], onehot, NN)

    state_ids = lax.broadcasted_iota(I32, (1, STATES), 1)
    for slot in range(GEN_DEV):
        g = order[slot]
        levels[slot : slot + 1, :] = level[pl.ds(g, 1), :]
        costs[slot : slot + 1, :] = jnp.where(state_ids < counts[g], cost[pl.ds(g, 1), :], 1e4)

    chunk = 256
    for slot in range(GEN_DEV):
        g = order[slot]
        span = STATES if slot < BIG_DEV else SMALL
        table = op_big.at[slot] if slot < BIG_DEV else op_small.at[slot - BIG_DEV]
        targets = [trans[j, pl.ds(g, 1), :span].astype(jnp.int16) for j in range(3)]

        def build(part, carry, targets=targets, span=span, table=table):
            start = pl.multiple_of(part * chunk, chunk)
            ids = (lax.broadcasted_iota(I32, (chunk, span), 0) + start).astype(jnp.int16)
            hits = [jnp.where(target == ids, BF16(1.0), BF16(0.0)) for target in targets]
            table[pl.ds(start, chunk), :] = hits[0] + hits[1] + hits[2]
            return carry

        lax.fori_loop(0, span // chunk, build, 0)

    def span_of(slot):
        return STATES if slot < BIG_DEV else SMALL

    def operator(slot):
        return op_big[slot] if slot < BIG_DEV else op_small[slot - BIG_DEV]

    def turned(slot):
        return turned_big[slot] if slot < BIG_DEV else turned_small[slot - BIG_DEV]

    def turn(slot):
        if slot < BIG_DEV:
            turned_big[slot] = op_big[slot].T
        else:
            turned_small[slot - BIG_DEV] = op_small[slot - BIG_DEV].T

    def hour_price(hour):
        return prices[pl.ds(pl.multiple_of(hour * SCN, SCN), SCN), :]

    def weight(slot, price_now):
        span = span_of(slot)
        return jnp.exp(
            price_now[:, slot : slot + 1] * levels[slot : slot + 1, :span] - costs[slot : slot + 1, :span]
        )

    def unit(value):
        return value * (1.0 / jnp.sum(value, axis=1, keepdims=True))

    def step_forward(slot, price_now):
        raised = dot(fwd_now[slot, :, : span_of(slot)], turned(slot), NN) * weight(slot, price_now)
        state = unit(raised)
        fwd_now[slot, :, : span_of(slot)] = state.astype(BF16)
        return state

    def step_backward(slot, price_now):
        back = dot(bwd_now[slot, :, : span_of(slot)], operator(slot), NN)
        bwd_now[slot, :, : span_of(slot)] = unit(back * weight(slot, price_now)).astype(BF16)
        return back

    first, last = hour_price(0), hour_price(HOURS - 1)
    for slot in range(GEN_DEV):
        span = span_of(slot)
        turn(slot)
        state = unit(weight(slot, first))
        fwd[0, slot, :, :span] = state
        fwd_now[slot, :, :span] = state.astype(BF16)
        bwd[0, slot, :, :span] = jnp.ones((SCN, span), F32)
        bwd_now[slot, :, :span] = unit(weight(slot, last)).astype(BF16)

    def early(k, carry):
        clear(k)
        price_f, price_b = hour_price(k), hour_price(HOURS - 1 - k)
        for slot in range(GEN_DEV):
            span = span_of(slot)
            fwd[k, slot, :, :span] = step_forward(slot, price_f)
            bwd[k, slot, :, :span] = step_backward(slot, price_b)
        return carry

    lanes = lax.broadcasted_iota(I32, (SCN, BLK), 1)

    def mean_level(slot, state, back):
        combined = state * back
        span = span_of(slot)
        top = jnp.sum(combined * levels[slot : slot + 1, :span], axis=1, keepdims=True)
        return top / jnp.sum(combined, axis=1, keepdims=True)

    result[0] = jnp.zeros((SCN, BLK), F32)
    result[1] = jnp.broadcast_to(sent_offsets, (SCN, BLK))

    def late(k, carry):
        invert(k - HOURS // 2)
        other = HOURS - 1 - k
        price_f, price_b = hour_price(k), hour_price(other)
        at_k = jnp.zeros((SCN, BLK), F32)
        at_other = jnp.zeros((SCN, BLK), F32)
        lanes_k = lanes - lax.rem(k, 8) * GEN_DEV
        lanes_other = lanes - other * GEN_DEV
        for slot in range(GEN_DEV):
            span = span_of(slot)
            state = step_forward(slot, price_f)
            back = step_backward(slot, price_b)
            at_k = jnp.where(lanes_k == slot, mean_level(slot, state, bwd[other, slot, :, :span]), at_k)
            at_other = jnp.where(lanes_other == slot, mean_level(slot, fwd[other, slot, :, :span], back), at_other)
        result[lax.div(k, 8)] += at_k
        result[0] += at_other
        return carry

    half = HOURS // 2
    lax.fori_loop(1, half, early, 0)
    lax.fori_loop(half, HOURS, late, 0)

    for owner in range(NGEN):
        rows = slice(owner * SCN_DEV, (owner + 1) * SCN_DEV)
        for part in range(2):
            out[owner, part * SCN_DEV : (part + 1) * SCN_DEV, :] = result[part, rows, :]


def plan(counts, gen_bus, pattern, trans, level, cost, price):
    vmem = pl.BlockSpec(memory_space=pltpu.VMEM)
    smem = pl.BlockSpec(memory_space=pltpu.SMEM)
    half = HOURS // 2
    return pl.pallas_call(
        plan_kernel,
        name="plan",
        out_shape=(
            jax.ShapeDtypeStruct((NGEN, 2 * SCN_DEV, BLK), F32),
            jax.ShapeDtypeStruct((LINE_BLKS, NX * NZ * 4), I32),
        ),
        in_specs=[smem, smem, smem, vmem, vmem, vmem, vmem],
        out_specs=(vmem, smem),
        scratch_shapes=[
            pltpu.SMEM((GEN_DEV,), I32),
            pltpu.VMEM((HOURS * SCN, BLK), F32),
            pltpu.VMEM((GEN_DEV, STATES), F32),
            pltpu.VMEM((GEN_DEV, STATES), F32),
            pltpu.VMEM((BIG_DEV, STATES, STATES), BF16),
            pltpu.VMEM((GEN_DEV - BIG_DEV, SMALL, SMALL), BF16),
            pltpu.VMEM((BIG_DEV, STATES, STATES), BF16),
            pltpu.VMEM((GEN_DEV - BIG_DEV, SMALL, SMALL), BF16),
            pltpu.VMEM((half, GEN_DEV, SCN, STATES), F32),
            pltpu.VMEM((half, GEN_DEV, SCN, STATES), F32),
            pltpu.VMEM((GEN_DEV, SCN, STATES), BF16),
            pltpu.VMEM((GEN_DEV, SCN, STATES), BF16),
            pltpu.VMEM((2, SCN, BLK), F32),
        ],
        compiler_params=pltpu.CompilerParams(vmem_limit_bytes=VMEM_LIMIT),
    )(counts, gen_bus, pattern, trans, level, cost, price)


class Links:
    def __init__(self, send, recv):
        self.send, self.recv, self.used, self.copies = send, recv, 0, {}
        self.x = lax.div(lax.axis_index("bus"), NZ)
        self.z = lax.rem(lax.axis_index("bus"), NZ)
        self.g = lax.axis_index("gen")

    def xs(self, step):
        return lax.rem(self.x + step + NX, NX)

    def zs(self, step):
        return lax.rem(self.z + step + NZ, NZ)

    def gs(self, step):
        return lax.rem(self.g + step + NGEN, NGEN)

    def along_x(self, step):
        return {"bus": self.xs(step) * NZ + self.z}

    def along_z(self, step):
        return {"bus": self.x * NZ + self.zs(step)}

    def along_gen(self, step):
        return {"gen": self.gs(step)}

    def start(self, key, src, dst, target):
        index = self.used
        self.used += 1
        copy = pltpu.make_async_remote_copy(
            src_ref=src,
            dst_ref=dst,
            send_sem=self.send.at[index],
            recv_sem=self.recv.at[index],
            device_id=target,
            device_id_type=MESH,
        )
        copy.start()
        assert key not in self.copies
        self.copies[key] = copy

    def arrived(self, key):
        self.copies[key].wait_recv()

    def drain(self):
        for copy in self.copies.values():
            copy.wait_send()


def greet(targets):
    barrier = pltpu.get_barrier_semaphore()
    for target in targets:
        pl.semaphore_signal(barrier, inc=1, device_id=target, device_id_type=MESH)
    pl.semaphore_wait(barrier, len(targets))


def take_turns(*routines):
    waiting = list(routines)
    while waiting:
        for routine in list(waiting):
            if next(routine, "over") == "over":
                waiting.remove(routine)


def gather_z_first(net, buf):
    def block(dx, dz):
        return buf.at[net.xs(dx), net.zs(dz)]

    def pass_on(dz):
        for i in (1, -1, 2):
            net.start(("Ax", i, dz), block(0, dz), block(0, dz), net.along_x(i))

    for dz in (4, 3, -3, 2, -2, 1, -1):
        net.start(("Az", dz), block(0, 0), block(0, 0), net.along_z(dz))
    pass_on(0)
    yield
    for group in ((1, -1), (2, -2), (3, -3), (4,)):
        for dz in group:
            net.arrived(("Az", dz))
            pass_on(-dz)
        yield
    for dz in (0, -1, 1, -2, 2, -3, 3, -4):
        for i in (1, -1, 2):
            net.arrived(("Ax", i, dz))


def gather_x_first(net, buf):
    def block(dx, dz):
        return buf.at[net.xs(dx), net.zs(dz)]

    def first(dx):
        for i in (2, -2, 1, -1):
            net.start(("Bz", dx, i), block(dx, 0), block(dx, 0), net.along_z(i))

    def second(dx):
        for i in (2, -2):
            near = i // 2
            c = 0 if i > 0 else 1
            net.arrived(("Bz", dx, i))
            net.start(("Bz4", dx, i), block(dx, -i).at[c], block(dx, -i).at[c], net.along_z(i))
            net.start(("Bz3", dx, i), block(dx, -i), block(dx, -i), net.along_z(near))

    for i in (2, 1, -1):
        net.start(("Bx", i), block(0, 0), block(0, 0), net.along_x(i))
    first(0)
    yield
    for i in (-1, 1, 2):
        net.arrived(("Bx", i))
        first(-i)
    yield
    second(0)
    yield
    second(1)
    second(-1)
    yield
    second(-2)
    yield
    for dx in (0, 1, -1, -2):
        for i in (1, -1):
            net.arrived(("Bz", dx, i))
        for i in (2, -2):
            net.arrived(("Bz3", dx, i))
            net.arrived(("Bz4", dx, i))


def wide(value):
    return value.astype(F32)


def reduce_x_first(net, part, along_x, to_z, arrived, kept, final):
    far_first = (4, 3, 5, 2, 6, 1, 7, 0)
    for dz in far_first:
        for n, i in enumerate((2, 1, -1)):
            net.start(("sum Ax", n, dz), part.at[net.xs(i), net.zs(dz)], along_x.at[n, dz], net.along_x(i))
    yield
    yield
    for dz in far_first:
        value = wide(part[net.x, net.zs(dz)])
        for n in range(3):
            net.arrived(("sum Ax", n, dz))
            value = value + wide(along_x[n, dz])
        if dz:
            to_z[dz] = value.astype(BF16)
            net.start(("sum Az", dz), to_z.at[dz], arrived.at[dz], net.along_z(dz))
        else:
            kept[...] = value
        if dz in (5, 6):
            yield
    yield
    value = kept[...]
    for dz in (1, 7, 2, 6, 3, 5, 4):
        net.arrived(("sum Az", dz))
        value = value + wide(arrived[dz])
    final[...] = value.astype(BF16)
    yield from spread_result(net, 0)


def reduce_z_first(net, part, near, third, fourth, to_two, from_two, to_x, arrived, kept, final):
    columns = (2, 1, 3, 0)
    for dx in columns:
        column = net.xs(dx)
        for n, i in enumerate((1, -1)):
            net.start(("sum B4", dx, n), part.at[column, net.zs(4), n], fourth.at[dx, n], net.along_z(2 * i))
            net.start(("sum B3", dx, n), part.at[column, net.zs(3 * i)], third.at[dx, n], net.along_z(i))
    for dx in columns:
        for n, i in enumerate((1, -1)):
            net.start(("sum B1", dx, n), part.at[net.xs(dx), net.zs(i)], near.at[dx, n], net.along_z(i))
    yield
    for dx in columns:
        for n, i in enumerate((1, -1)):
            net.arrived(("sum B3", dx, n))
            net.arrived(("sum B4", dx, n))
            value = wide(part[net.xs(dx), net.zs(2 * i)]) + wide(third[dx, n])
            to_two[dx, n, 1 - n] = value[1 - n].astype(BF16)
            to_two[dx, n, n] = (value[n] + wide(fourth[dx, n])).astype(BF16)
            net.start(("sum B2", dx, n), to_two.at[dx, n], from_two.at[dx, n], net.along_z(2 * i))
        if dx in (2, 3):
            yield
    yield
    for dx in columns:
        value = wide(part[net.xs(dx), net.z])
        for n in range(2):
            net.arrived(("sum B1", dx, n))
            net.arrived(("sum B2", dx, n))
            value = value + (wide(near[dx, n]) + wide(from_two[dx, n]))
        if dx:
            to_x[dx] = value.astype(BF16)
            net.start(("sum Bx", dx), to_x.at[dx], arrived.at[dx], net.along_x(dx))
        else:
            kept[...] = value
    yield
    value = kept[...]
    for dx in (1, 3, 2):
        net.arrived(("sum Bx", dx))
        value = value + wide(arrived[dx])
    final[...] = value.astype(BF16)
    yield from spread_result(net, 1)


def spread_result(net, half):
    for i in range(1, NGEN):
        mine = net.finals.at[net.g, half]
        net.start(("out", half, i), mine, mine, net.along_gen(i))
    yield


NET_COPIES = 7 + 31 + 35 + 31 + 35 + 14


def place_of(block):
    device, c = lax.div(block, 4), lax.rem(block, 4)
    return (lax.div(c, 2) * (NX * NZ) + device) * 2 + lax.rem(c, 2)


def network_kernel(
    pattern,
    inverse,
    generation,
    demand,
    mult,
    limits,
    ptdf_far,
    finals,
    new_mult,
    peers,
    netf,
    nets,
    ptdf,
    changes,
    spreads,
    shares,
    a_x,
    a_to_z,
    a_arrived,
    a_kept,
    b_near,
    b_third,
    b_fourth,
    b_to_two,
    b_from_two,
    b_to_x,
    b_arrived,
    b_kept,
    send,
    recv,
    done,
):
    net = Links(send, recv)
    net.finals = finals
    load_ptdf = pltpu.make_async_copy(ptdf_far, ptdf, done)
    load_ptdf.start()
    greet(
        [net.along_x(i) for i in range(1, NX)]
        + [net.along_z(i) for i in range(1, NZ)]
        + [net.along_gen(i) for i in range(1, NGEN)]
    )

    for i in range(1, NGEN):
        net.start(("gen", i), generation.at[net.gs(i)], peers.at[net.g], net.along_gen(i))
    peers[net.g] = generation[net.g]
    for i in range(1, NGEN):
        net.arrived(("gen", i))
    lane_group = lax.div(lax.broadcasted_iota(I32, (2 * SCN_DEV, BLK), 1), GEN_DEV)
    by_hour = [jnp.zeros((2 * SCN_DEV, BLK), F32) for hour in range(8)]
    for source in range(NGEN):
        packed = peers[source]
        for hour in range(8):
            moved = pltpu.roll(packed, (source - hour) % NGEN * GEN_DEV, 1) if source != hour else packed
            by_hour[hour] = jnp.where(lane_group == source, moved, by_hour[hour])
    hours = [by_hour[t % 8][t // 8 * SCN_DEV : (t // 8 + 1) * SCN_DEV, :] for t in range(HOURS)]
    offsets = by_hour[HOURS % 8][SCN_DEV : SCN_DEV + 1, :]
    total = jnp.concatenate(hours, axis=0)

    spots = wide(lax.broadcasted_iota(I32, (BUS_DEV, BLK), 0))
    onehot = (spots == offsets).astype(BF16)
    high, middle, low = split3(total)
    netf[...] = dot(high, onehot, NT) + dot(middle, onehot, NT) + dot(low, onehot, NT)
    for t in range(HOURS):
        netf[t * SCN_DEV : (t + 1) * SCN_DEV, :] -= demand[t]
    rounded = netf[...].astype(BF16)
    for half in range(2):
        for c in range(2):
            column = (half * 2 + c) * BLK
            nets[half, net.x, net.z, c] = rounded[:, column : column + BLK]

    take_turns(gather_z_first(net, nets.at[0]), gather_x_first(net, nets.at[1]))

    load_ptdf.wait()
    blocks = nets.reshape(2 * NX * NZ * 2, ROWS, BLK)
    spreads[LINE_BLKS * NNZB] = jnp.zeros((ROWS, BLK), F32)
    for line in range(LINE_BLKS):
        lanes = slice(line * BLK, (line + 1) * BLK)
        places = [place_of(pattern[line, j]) for j in range(NNZB)]
        flow = jnp.zeros((ROWS, BLK), F32)
        for j in range(0, NNZB, 2):
            pair = jnp.concatenate([blocks[places[j]], blocks[places[j + 1]]], axis=1)
            flow = flow + dot(pair, ptdf[line, j : j + 2].reshape(2 * BLK, BLK), NN)
        limit = limits[lanes].reshape(1, BLK)
        for t in range(HOURS):
            rows = slice(t * SCN_DEV, (t + 1) * SCN_DEV)
            here = flow[rows, :]
            upper_old, lower_old = mult[0, t, :, lanes], mult[1, t, :, lanes]
            upper = jnp.maximum(0.0, upper_old + (here - limit))
            lower = jnp.maximum(0.0, lower_old + (-here - limit))
            new_mult[0, t, :, lanes] = upper
            new_mult[1, t, :, lanes] = lower
            changes[rows, :] = (upper - upper_old) - (lower - lower_old)
        change = changes[...].astype(BF16)
        spread = dot(change, ptdf[line].reshape(NNZB * BLK, BLK), NT)
        for j in range(NNZB):
            spreads[line * NNZB + j] = spread[:, j * BLK : (j + 1) * BLK]

    def collect(device, carry):
        x, z = lax.div(device, NZ), lax.rem(device, NZ)
        for half in range(2):
            for c in range(2):
                block = device * 4 + half * 2 + c
                value = spreads[inverse[0, block]]
                for line in range(1, LINE_BLKS):
                    value = value + spreads[inverse[line, block]]
                shares[half, x, z, c] = value.astype(BF16)
        return carry

    lax.fori_loop(0, NX * NZ, collect, 0)

    take_turns(
        reduce_x_first(net, shares.at[0], a_x, a_to_z, a_arrived, a_kept, finals.at[net.g, 0]),
        reduce_z_first(
            net,
            shares.at[1],
            b_near,
            b_third,
            b_fourth,
            b_to_two,
            b_from_two,
            b_to_x,
            b_arrived,
            b_kept,
            finals.at[net.g, 1],
        ),
    )
    for half in range(2):
        for i in range(1, NGEN):
            net.arrived(("out", half, i))
    net.drain()


def network(pattern, inverse, generation, demand, mult, limits, ptdf):
    vmem = pl.BlockSpec(memory_space=pltpu.VMEM)
    smem = pl.BlockSpec(memory_space=pltpu.SMEM)
    far = pl.BlockSpec(memory_space=pl.ANY)
    piece = (2, ROWS, BLK)
    everything = (2, NX, NZ) + piece
    return pl.pallas_call(
        network_kernel,
        name="network",
        out_shape=(
            jax.ShapeDtypeStruct((NGEN, 2) + piece, BF16),
            jax.ShapeDtypeStruct(mult.shape, F32),
        ),
        in_specs=[smem, smem, vmem, vmem, vmem, vmem, far],
        out_specs=(vmem, vmem),
        scratch_shapes=[
            pltpu.VMEM(generation.shape, F32),
            pltpu.VMEM((ROWS, BUS_DEV), F32),
            pltpu.VMEM(everything, BF16),
            pltpu.VMEM(ptdf.shape, BF16),
            pltpu.VMEM((ROWS, BLK), F32),
            pltpu.VMEM((LINE_BLKS * NNZB + 1, ROWS, BLK), F32),
            pltpu.VMEM(everything, BF16),
            pltpu.VMEM((3, NZ) + piece, BF16),
            pltpu.VMEM((NZ,) + piece, BF16),
            pltpu.VMEM((NZ,) + piece, BF16),
            pltpu.VMEM(piece, F32),
            pltpu.VMEM((NX, 2) + piece, BF16),
            pltpu.VMEM((NX, 2) + piece, BF16),
            pltpu.VMEM((NX, 2, ROWS, BLK), BF16),
            pltpu.VMEM((NX, 2) + piece, BF16),
            pltpu.VMEM((NX, 2) + piece, BF16),
            pltpu.VMEM((NX,) + piece, BF16),
            pltpu.VMEM((NX,) + piece, BF16),
            pltpu.VMEM(piece, F32),
            pltpu.SemaphoreType.DMA((NET_COPIES,)),
            pltpu.SemaphoreType.DMA((NET_COPIES,)),
            pltpu.SemaphoreType.DMA,
        ],
        compiler_params=pltpu.CompilerParams(
            collective_id=0, has_side_effects=True, vmem_limit_bytes=VMEM_LIMIT
        ),
    )(pattern, inverse, generation, demand, mult, limits, ptdf)


def finish_kernel(finals, price, mult, new_price, new_mult):
    for owner in range(NGEN):
        scenarios = slice(owner * SCN_DEV, (owner + 1) * SCN_DEV)
        for block in range(4):
            columns = slice(block * BLK, (block + 1) * BLK)
            change = wide(finals[owner, block // 2, block % 2])
            for t in range(HOURS):
                new_price[t, scenarios, columns] = (
                    price[t, scenarios, columns] - change[t * SCN_DEV : (t + 1) * SCN_DEV, :]
                )
    new_mult[...] = mult[...]


def finish(finals, price, mult):
    vmem = pl.BlockSpec(memory_space=pltpu.VMEM)
    return pl.pallas_call(
        finish_kernel,
        name="finish",
        out_shape=(jax.ShapeDtypeStruct(price.shape, F32), jax.ShapeDtypeStruct(mult.shape, F32)),
        in_specs=[vmem] * 3,
        out_specs=(vmem, vmem),
        compiler_params=pltpu.CompilerParams(vmem_limit_bytes=VMEM_LIMIT),
    )(finals, price, mult)


def shards(
    bus_price,
    bus_demand,
    multipliers,
    line_limits,
    ptdf_blocks,
    ptdf_pattern,
    gen_bus,
    state_counts,
    transitions,
    state_level,
    state_cost,
):
    price = bus_price.transpose(1, 0, 2)
    generation, inverse = plan(
        state_counts, gen_bus, ptdf_pattern, transitions.transpose(1, 0, 2), state_level, state_cost, price
    )
    finals, mult = network(
        ptdf_pattern,
        inverse,
        generation,
        bus_demand.transpose(1, 0, 2),
        multipliers.transpose(0, 2, 1, 3),
        line_limits,
        ptdf_blocks,
    )
    new_price, new_mult = finish(finals, price, mult)
    return new_mult.transpose(0, 2, 1, 3), new_price.transpose(1, 0, 2)


def solution(mesh):
    in_specs = (
        P(None, None, "bus"),
        P("gen", None, "bus"),
        P(None, "gen", None, "bus"),
        P("bus"),
        P("bus", None, None, None),
        P("bus", None),
        P(("gen", "bus")),
        P(("gen", "bus")),
        P(("gen", "bus"), None, None),
        P(("gen", "bus"), None),
        P(("gen", "bus"), None),
    )
    out_specs = (P(None, "gen", None, "bus"), P(None, None, "bus"))
    return jax.shard_map(shards, mesh=mesh, in_specs=in_specs, out_specs=out_specs, check_vma=False)
```

```python
import functools

import jax
import jax.numpy as jnp
from jax import lax
from jax.experimental import pallas as pl
from jax.experimental.pallas import tpu as pltpu
from jax.sharding import PartitionSpec as P

STATES = 512
SMALL = 256
BIG_DEV = 6
GEN_DEV = 16
BLK = 128
NNZB = 16
HOURS = 12
SCN = 32
SCN_DEV = 4
ROWS = SCN_DEV * HOURS
BUS_DEV = 512
NX, NZ, NGEN = 4, 8, 8
LINE_BLKS = 6
F32, BF16, I32 = jnp.float32, jnp.bfloat16, jnp.int32
MESH = pl.DeviceIdType.MESH
NN = (((1,), (0,)), ((), ()))
NT = (((1,), (1,)), ((), ()))
OFFSET_LANE = (HOURS % 8) * GEN_DEV
VMEM_LIMIT = 58 * 1024 * 1024


def dot(a, b, dims):
    return lax.dot_general(a, b, dims, preferred_element_type=F32)


def split3(value):
    high = value.astype(BF16)
    rest = value - high.astype(F32)
    middle = rest.astype(BF16)
    low = (rest - middle.astype(F32)).astype(BF16)
    return high, middle, low


def plan_steps(
    counts,
    gen_bus,
    pattern,
    trans,
    level,
    cost,
    price,
    out,
    inverse,
    order,
    table_now,
    table_done,
    prices,
    levels,
    costs,
    op_big,
    op_small,
    turned_big,
    turned_small,
    fwd,
    bwd,
    fwd_now,
    bwd_now,
    result,
):
    big_so_far = jnp.int32(0)
    slots = []
    for g in range(GEN_DEV):
        big = (counts[g] > SMALL).astype(I32)
        slots.append(jnp.where(big == 1, big_so_far, GEN_DEV - 1 - (g - big_so_far)))
        big_so_far = big_so_far + big
    for slot in range(GEN_DEV):
        holder = jnp.int32(0)
        for g in range(1, GEN_DEV):
            holder = holder + jnp.where(slots[g] == slot, g, 0)
        order[slot] = holder

    block_ids = lax.broadcasted_iota(I32, (1, NX * NZ * 4), 1)
    for line in range(LINE_BLKS):
        row = jnp.full((1, NX * NZ * 4), LINE_BLKS * NNZB, I32)
        for j in range(NNZB):
            row = jnp.where(block_ids == pattern[line, j], line * NNZB + j, row)
        table_now[line : line + 1, :] = row
    copy_table = pltpu.make_async_copy(table_now, inverse, table_done)
    copy_table.start()

    lane = lax.broadcasted_iota(I32, (1, BLK), 1)
    offset_row = jnp.full((1, BLK), -1, I32)
    sent_offsets = jnp.zeros((1, BLK), F32)
    for slot in range(GEN_DEV):
        offset = lax.rem(gen_bus[order[slot]], BUS_DEV)
        offset_row = jnp.where(lane == slot, offset, offset_row)
        sent_offsets = jnp.where(lane == OFFSET_LANE + slot, offset.astype(F32), sent_offsets)

    onehot = (lax.broadcasted_iota(I32, (BUS_DEV, BLK), 0) == offset_row).astype(BF16)
    pieces = split3(price[...].reshape(HOURS * SCN, BUS_DEV))
    prices[...] = dot(pieces[0], onehot, NN) + dot(pieces[1], onehot, NN) + dot(pieces[2], onehot, NN)

    state_ids = lax.broadcasted_iota(I32, (1, STATES), 1)
    for slot in range(GEN_DEV):
        g = order[slot]
        levels[slot : slot + 1, :] = level[pl.ds(g, 1), :]
        costs[slot : slot + 1, :] = jnp.where(state_ids < counts[g], cost[pl.ds(g, 1), :], 1e4)

    chunk = 256
    for slot in range(GEN_DEV):
        g = order[slot]
        span = STATES if slot < BIG_DEV else SMALL
        table = op_big.at[slot] if slot < BIG_DEV else op_small.at[slot - BIG_DEV]
        targets = [trans[j, pl.ds(g, 1), :span].astype(jnp.int16) for j in range(3)]

        def build(part, carry, targets=targets, span=span, table=table):
            start = pl.multiple_of(part * chunk, chunk)
            ids = (lax.broadcasted_iota(I32, (chunk, span), 0) + start).astype(jnp.int16)
            hits = [jnp.where(target == ids, BF16(1.0), BF16(0.0)) for target in targets]
            table[pl.ds(start, chunk), :] = hits[0] + hits[1] + hits[2]
            return carry

        lax.fori_loop(0, span // chunk, build, 0)

    def span_of(slot):
        return STATES if slot < BIG_DEV else SMALL

    def operator(slot):
        return op_big[slot] if slot < BIG_DEV else op_small[slot - BIG_DEV]

    def turned(slot):
        return turned_big[slot] if slot < BIG_DEV else turned_small[slot - BIG_DEV]

    def turn(slot):
        if slot < BIG_DEV:
            turned_big[slot] = op_big[slot].T
        else:
            turned_small[slot - BIG_DEV] = op_small[slot - BIG_DEV].T

    def hour_price(hour):
        return prices[pl.ds(pl.multiple_of(hour * SCN, SCN), SCN), :]

    def weight(slot, price_now):
        span = span_of(slot)
        return jnp.exp(
            price_now[:, slot : slot + 1] * levels[slot : slot + 1, :span] - costs[slot : slot + 1, :span]
        )

    def unit(value):
        return value * (1.0 / jnp.sum(value, axis=1, keepdims=True))

    def step_forward(slot, price_now):
        raised = dot(fwd_now[slot, :, : span_of(slot)], turned(slot), NN) * weight(slot, price_now)
        state = unit(raised)
        fwd_now[slot, :, : span_of(slot)] = state.astype(BF16)
        return state

    def step_backward(slot, price_now):
        back = dot(bwd_now[slot, :, : span_of(slot)], operator(slot), NN)
        bwd_now[slot, :, : span_of(slot)] = unit(back * weight(slot, price_now)).astype(BF16)
        return back

    first, last = hour_price(0), hour_price(HOURS - 1)
    for slot in range(GEN_DEV):
        span = span_of(slot)
        turn(slot)
        state = unit(weight(slot, first))
        fwd[0, slot, :, :span] = state
        fwd_now[slot, :, :span] = state.astype(BF16)
        bwd[0, slot, :, :span] = jnp.ones((SCN, span), F32)
        bwd_now[slot, :, :span] = unit(weight(slot, last)).astype(BF16)

    def early(k, carry):
        price_f, price_b = hour_price(k), hour_price(HOURS - 1 - k)
        for slot in range(GEN_DEV):
            span = span_of(slot)
            fwd[k, slot, :, :span] = step_forward(slot, price_f)
            bwd[k, slot, :, :span] = step_backward(slot, price_b)
        return carry

    lanes = lax.broadcasted_iota(I32, (SCN, BLK), 1)

    def mean_level(slot, state, back):
        combined = state * back
        span = span_of(slot)
        top = jnp.sum(combined * levels[slot : slot + 1, :span], axis=1, keepdims=True)
        return top / jnp.sum(combined, axis=1, keepdims=True)

    result[0] = jnp.zeros((SCN, BLK), F32)
    result[1] = jnp.broadcast_to(sent_offsets, (SCN, BLK))

    def late(k, carry):
        other = HOURS - 1 - k
        price_f, price_b = hour_price(k), hour_price(other)
        at_k = jnp.zeros((SCN, BLK), F32)
        at_other = jnp.zeros((SCN, BLK), F32)
        lanes_k = lanes - lax.rem(k, 8) * GEN_DEV
        lanes_other = lanes - other * GEN_DEV
        for slot in range(GEN_DEV):
            span = span_of(slot)
            state = step_forward(slot, price_f)
            back = step_backward(slot, price_b)
            at_k = jnp.where(lanes_k == slot, mean_level(slot, state, bwd[other, slot, :, :span]), at_k)
            at_other = jnp.where(lanes_other == slot, mean_level(slot, fwd[other, slot, :, :span], back), at_other)
        result[lax.div(k, 8)] += at_k
        result[0] += at_other
        return carry

    half = HOURS // 2
    lax.fori_loop(1, half, early, 0)
    lax.fori_loop(half, HOURS, late, 0)

    copy_table.wait()
    for owner in range(NGEN):
        rows = slice(owner * SCN_DEV, (owner + 1) * SCN_DEV)
        for part in range(2):
            out[owner, part * SCN_DEV : (part + 1) * SCN_DEV, :] = result[part, rows, :]


def plan_scratch():
    half = HOURS // 2
    return [
        pltpu.VMEM((NGEN, 2 * SCN_DEV, BLK), F32),
        pltpu.SMEM((8, NX * NZ * 4), I32),
        pltpu.SMEM((GEN_DEV,), I32),
        pltpu.VMEM((8, NX * NZ * 4), I32),
        pltpu.SemaphoreType.DMA,
        pltpu.VMEM((HOURS * SCN, BLK), F32),
        pltpu.VMEM((GEN_DEV, STATES), F32),
        pltpu.VMEM((GEN_DEV, STATES), F32),
        pltpu.VMEM((BIG_DEV, STATES, STATES), BF16),
        pltpu.VMEM((GEN_DEV - BIG_DEV, SMALL, SMALL), BF16),
        pltpu.VMEM((BIG_DEV, STATES, STATES), BF16),
        pltpu.VMEM((GEN_DEV - BIG_DEV, SMALL, SMALL), BF16),
        pltpu.VMEM((half, GEN_DEV, SCN, STATES), F32),
        pltpu.VMEM((half, GEN_DEV, SCN, STATES), F32),
        pltpu.VMEM((GEN_DEV, SCN, STATES), BF16),
        pltpu.VMEM((GEN_DEV, SCN, STATES), BF16),
        pltpu.VMEM((2, SCN, BLK), F32),
    ]


class Links:
    def __init__(self, send, recv):
        self.send, self.recv, self.used, self.copies = send, recv, 0, {}
        self.x = lax.div(lax.axis_index("bus"), NZ)
        self.z = lax.rem(lax.axis_index("bus"), NZ)
        self.g = lax.axis_index("gen")

    def xs(self, step):
        return lax.rem(self.x + step + NX, NX)

    def zs(self, step):
        return lax.rem(self.z + step + NZ, NZ)

    def gs(self, step):
        return lax.rem(self.g + step + NGEN, NGEN)

    def along_x(self, step):
        return {"bus": self.xs(step) * NZ + self.z}

    def along_z(self, step):
        return {"bus": self.x * NZ + self.zs(step)}

    def along_gen(self, step):
        return {"gen": self.gs(step)}

    def start(self, key, src, dst, target):
        index = self.used
        self.used += 1
        copy = pltpu.make_async_remote_copy(
            src_ref=src,
            dst_ref=dst,
            send_sem=self.send.at[index],
            recv_sem=self.recv.at[index],
            device_id=target,
            device_id_type=MESH,
        )
        copy.start()
        assert key not in self.copies
        self.copies[key] = copy

    def arrived(self, key):
        self.copies[key].wait_recv()

    def drain(self):
        for copy in self.copies.values():
            copy.wait_send()


def greet(targets):
    barrier = pltpu.get_barrier_semaphore()
    for target in targets:
        pl.semaphore_signal(barrier, inc=1, device_id=target, device_id_type=MESH)
    return functools.partial(pl.semaphore_wait, barrier, len(targets))


def take_turns(*routines):
    waiting = list(routines)
    while waiting:
        for routine in list(waiting):
            if next(routine, "over") == "over":
                waiting.remove(routine)


def gather_z_first(net, buf):
    def block(dx, dz):
        return buf.at[net.xs(dx), net.zs(dz)]

    def pass_on(dz):
        for i in (1, -1, 2):
            net.start(("Ax", i, dz), block(0, dz), block(0, dz), net.along_x(i))

    for dz in (4, 3, -3, 2, -2, 1, -1):
        net.start(("Az", dz), block(0, 0), block(0, 0), net.along_z(dz))
    pass_on(0)
    yield
    for group in ((1, -1), (2, -2), (3, -3), (4,)):
        for dz in group:
            net.arrived(("Az", dz))
            pass_on(-dz)
        yield
    for dz in (0, -1, 1, -2, 2, -3, 3, -4):
        for i in (1, -1, 2):
            net.arrived(("Ax", i, dz))


def gather_x_first(net, buf):
    def block(dx, dz):
        return buf.at[net.xs(dx), net.zs(dz)]

    def first(dx):
        for i in (2, -2, 1, -1):
            net.start(("Bz", dx, i), block(dx, 0), block(dx, 0), net.along_z(i))

    def second(dx):
        for i in (2, -2):
            near = i // 2
            c = 0 if i > 0 else 1
            net.arrived(("Bz", dx, i))
            net.start(("Bz4", dx, i), block(dx, -i).at[c], block(dx, -i).at[c], net.along_z(i))
            net.start(("Bz3", dx, i), block(dx, -i), block(dx, -i), net.along_z(near))

    for i in (2, 1, -1):
        net.start(("Bx", i), block(0, 0), block(0, 0), net.along_x(i))
    first(0)
    yield
    for i in (-1, 1, 2):
        net.arrived(("Bx", i))
        first(-i)
    yield
    second(0)
    yield
    second(1)
    second(-1)
    yield
    second(-2)
    yield
    for dx in (0, 1, -1, -2):
        for i in (1, -1):
            net.arrived(("Bz", dx, i))
        for i in (2, -2):
            net.arrived(("Bz3", dx, i))
            net.arrived(("Bz4", dx, i))


def wide(value):
    return value.astype(F32)


def reduce_x_first(net, part, along_x, to_z, arrived, kept, final):
    far_first = (4, 3, 5, 2, 6, 1, 7, 0)
    for dz in far_first:
        for n, i in enumerate((2, 1, -1)):
            net.start(("sum Ax", n, dz), part.at[net.xs(i), net.zs(dz)], along_x.at[n, dz], net.along_x(i))
    yield
    yield
    for dz in far_first:
        value = wide(part[net.x, net.zs(dz)])
        for n in range(3):
            net.arrived(("sum Ax", n, dz))
            value = value + wide(along_x[n, dz])
        if dz:
            to_z[dz] = value.astype(BF16)
            net.start(("sum Az", dz), to_z.at[dz], arrived.at[dz], net.along_z(dz))
        else:
            kept[...] = value
        if dz in (5, 6):
            yield
    yield
    value = kept[...]
    for dz in (1, 7, 2, 6, 3, 5, 4):
        net.arrived(("sum Az", dz))
        value = value + wide(arrived[dz])
    final[...] = value.astype(BF16)
    yield from spread_result(net, 0)


def reduce_z_first(net, part, near, third, fourth, to_two, from_two, to_x, arrived, kept, final):
    columns = (2, 1, 3, 0)
    for dx in columns:
        column = net.xs(dx)
        for n, i in enumerate((1, -1)):
            net.start(("sum B4", dx, n), part.at[column, net.zs(4), n], fourth.at[dx, n], net.along_z(2 * i))
            net.start(("sum B3", dx, n), part.at[column, net.zs(3 * i)], third.at[dx, n], net.along_z(i))
    for dx in columns:
        for n, i in enumerate((1, -1)):
            net.start(("sum B1", dx, n), part.at[net.xs(dx), net.zs(i)], near.at[dx, n], net.along_z(i))
    yield
    for dx in columns:
        for n, i in enumerate((1, -1)):
            net.arrived(("sum B3", dx, n))
            net.arrived(("sum B4", dx, n))
            value = wide(part[net.xs(dx), net.zs(2 * i)]) + wide(third[dx, n])
            to_two[dx, n, 1 - n] = value[1 - n].astype(BF16)
            to_two[dx, n, n] = (value[n] + wide(fourth[dx, n])).astype(BF16)
            net.start(("sum B2", dx, n), to_two.at[dx, n], from_two.at[dx, n], net.along_z(2 * i))
        if dx in (2, 3):
            yield
    yield
    for dx in columns:
        value = wide(part[net.xs(dx), net.z])
        for n in range(2):
            net.arrived(("sum B1", dx, n))
            net.arrived(("sum B2", dx, n))
            value = value + (wide(near[dx, n]) + wide(from_two[dx, n]))
        if dx:
            to_x[dx] = value.astype(BF16)
            net.start(("sum Bx", dx), to_x.at[dx], arrived.at[dx], net.along_x(dx))
        else:
            kept[...] = value
    yield
    value = kept[...]
    for dx in (1, 3, 2):
        net.arrived(("sum Bx", dx))
        value = value + wide(arrived[dx])
    final[...] = value.astype(BF16)
    yield from spread_result(net, 1)


def spread_result(net, half):
    for i in range(1, NGEN):
        mine = net.finals.at[net.g, half]
        net.start(("out", half, i), mine, mine, net.along_gen(i))
    yield


NET_COPIES = 7 + 31 + 35 + 31 + 35 + 14


def place_of(block):
    device, c = lax.div(block, 4), lax.rem(block, 4)
    return (lax.div(c, 2) * (NX * NZ) + device) * 2 + lax.rem(c, 2)


def network_kernel(
    counts,
    gen_bus,
    pattern,
    trans,
    level,
    cost,
    price,
    demand,
    mult,
    limits,
    ptdf_far,
    finals,
    new_mult,
    peers,
    netf,
    nets,
    ptdf,
    changes,
    spreads,
    shares,
    a_x,
    a_to_z,
    a_arrived,
    a_kept,
    b_near,
    b_third,
    b_fourth,
    b_to_two,
    b_from_two,
    b_to_x,
    b_arrived,
    b_kept,
    send,
    recv,
    done,
    *plan_refs,
):
    net = Links(send, recv)
    net.finals = finals
    load_ptdf = pltpu.make_async_copy(ptdf_far, ptdf, done)
    load_ptdf.start()
    everyone_here = greet(
        [net.along_x(i) for i in range(1, NX)]
        + [net.along_z(i) for i in range(1, NZ)]
        + [net.along_gen(i) for i in range(1, NGEN)]
    )
    generation, inverse = plan_refs[0], plan_refs[1]
    plan_steps(counts, gen_bus, pattern, trans, level, cost, price, *plan_refs)
    everyone_here()

    for i in range(1, NGEN):
        net.start(("gen", i), generation.at[net.gs(i)], peers.at[net.g], net.along_gen(i))
    peers[net.g] = generation[net.g]
    for i in range(1, NGEN):
        net.arrived(("gen", i))
    lane_group = lax.div(lax.broadcasted_iota(I32, (2 * SCN_DEV, BLK), 1), GEN_DEV)
    by_hour = [jnp.zeros((2 * SCN_DEV, BLK), F32) for hour in range(8)]
    for source in range(NGEN):
        packed = peers[source]
        for hour in range(8):
            moved = pltpu.roll(packed, (source - hour) % NGEN * GEN_DEV, 1) if source != hour else packed
            by_hour[hour] = jnp.where(lane_group == source, moved, by_hour[hour])
    hours = [by_hour[t % 8][t // 8 * SCN_DEV : (t // 8 + 1) * SCN_DEV, :] for t in range(HOURS)]
    offsets = by_hour[HOURS % 8][SCN_DEV : SCN_DEV + 1, :]
    total = jnp.concatenate(hours, axis=0)

    spots = wide(lax.broadcasted_iota(I32, (BUS_DEV, BLK), 0))
    onehot = (spots == offsets).astype(BF16)
    high, middle, low = split3(total)
    netf[...] = dot(high, onehot, NT) + dot(middle, onehot, NT) + dot(low, onehot, NT)
    for t in range(HOURS):
        netf[t * SCN_DEV : (t + 1) * SCN_DEV, :] -= demand[t]
    rounded = netf[...].astype(BF16)
    for half in range(2):
        for c in range(2):
            column = (half * 2 + c) * BLK
            nets[half, net.x, net.z, c] = rounded[:, column : column + BLK]

    take_turns(gather_z_first(net, nets.at[0]), gather_x_first(net, nets.at[1]))

    load_ptdf.wait()
    blocks = nets.reshape(2 * NX * NZ * 2, ROWS, BLK)
    spreads[LINE_BLKS * NNZB] = jnp.zeros((ROWS, BLK), F32)
    for line in range(LINE_BLKS):
        lanes = slice(line * BLK, (line + 1) * BLK)
        places = [place_of(pattern[line, j]) for j in range(NNZB)]
        flow = jnp.zeros((ROWS, BLK), F32)
        for j in range(0, NNZB, 2):
            pair = jnp.concatenate([blocks[places[j]], blocks[places[j + 1]]], axis=1)
            flow = flow + dot(pair, ptdf[line, j : j + 2].reshape(2 * BLK, BLK), NN)
        limit = limits[lanes].reshape(1, BLK)
        for t in range(HOURS):
            rows = slice(t * SCN_DEV, (t + 1) * SCN_DEV)
            here = flow[rows, :]
            upper_old, lower_old = mult[0, t, :, lanes], mult[1, t, :, lanes]
            upper = jnp.maximum(0.0, upper_old + (here - limit))
            lower = jnp.maximum(0.0, lower_old + (-here - limit))
            new_mult[0, t, :, lanes] = upper
            new_mult[1, t, :, lanes] = lower
            changes[rows, :] = (upper - upper_old) - (lower - lower_old)
        change = changes[...].astype(BF16)
        spread = dot(change, ptdf[line].reshape(NNZB * BLK, BLK), NT)
        for j in range(NNZB):
            spreads[line * NNZB + j] = spread[:, j * BLK : (j + 1) * BLK]

    def collect(half, device, carry):
        x, z = lax.div(device, NZ), lax.rem(device, NZ)
        for c in range(2):
            block = device * 4 + half * 2 + c
            value = spreads[inverse[0, block]]
            for line in range(1, LINE_BLKS):
                value = value + spreads[inverse[line, block]]
            shares[half, x, z, c] = value.astype(BF16)
        return carry

    lax.fori_loop(0, NX * NZ, functools.partial(collect, 1), 0)
    longer = reduce_z_first(
        net,
        shares.at[1],
        b_near,
        b_third,
        b_fourth,
        b_to_two,
        b_from_two,
        b_to_x,
        b_arrived,
        b_kept,
        finals.at[net.g, 1],
    )
    next(longer)
    lax.fori_loop(0, NX * NZ, functools.partial(collect, 0), 0)
    shorter = reduce_x_first(net, shares.at[0], a_x, a_to_z, a_arrived, a_kept, finals.at[net.g, 0])
    next(shorter)
    take_turns(longer, shorter)
    for half in range(2):
        for i in range(1, NGEN):
            net.arrived(("out", half, i))
    net.drain()


def network(counts, gen_bus, pattern, trans, level, cost, price, demand, mult, limits, ptdf):
    vmem = pl.BlockSpec(memory_space=pltpu.VMEM)
    smem = pl.BlockSpec(memory_space=pltpu.SMEM)
    far = pl.BlockSpec(memory_space=pl.ANY)
    piece = (2, ROWS, BLK)
    everything = (2, NX, NZ) + piece
    return pl.pallas_call(
        network_kernel,
        name="network",
        out_shape=(
            jax.ShapeDtypeStruct((NGEN, 2) + piece, BF16),
            jax.ShapeDtypeStruct(mult.shape, F32),
        ),
        in_specs=[smem] * 3 + [vmem] * 7 + [far],
        out_specs=(vmem, vmem),
        scratch_shapes=[
            pltpu.VMEM((NGEN, 2 * SCN_DEV, BLK), F32),
            pltpu.VMEM((ROWS, BUS_DEV), F32),
            pltpu.VMEM(everything, BF16),
            pltpu.VMEM(ptdf.shape, BF16),
            pltpu.VMEM((ROWS, BLK), F32),
            pltpu.VMEM((LINE_BLKS * NNZB + 1, ROWS, BLK), F32),
            pltpu.VMEM(everything, BF16),
            pltpu.VMEM((3, NZ) + piece, BF16),
            pltpu.VMEM((NZ,) + piece, BF16),
            pltpu.VMEM((NZ,) + piece, BF16),
            pltpu.VMEM(piece, F32),
            pltpu.VMEM((NX, 2) + piece, BF16),
            pltpu.VMEM((NX, 2) + piece, BF16),
            pltpu.VMEM((NX, 2, ROWS, BLK), BF16),
            pltpu.VMEM((NX, 2) + piece, BF16),
            pltpu.VMEM((NX, 2) + piece, BF16),
            pltpu.VMEM((NX,) + piece, BF16),
            pltpu.VMEM((NX,) + piece, BF16),
            pltpu.VMEM(piece, F32),
            pltpu.SemaphoreType.DMA((NET_COPIES,)),
            pltpu.SemaphoreType.DMA((NET_COPIES,)),
            pltpu.SemaphoreType.DMA,
        ]
        + plan_scratch(),
        compiler_params=pltpu.CompilerParams(
            collective_id=0, has_side_effects=True, vmem_limit_bytes=VMEM_LIMIT
        ),
    )(counts, gen_bus, pattern, trans, level, cost, price, demand, mult, limits, ptdf)


def finish_kernel(finals, price, mult, new_price, new_mult):
    for owner in range(NGEN):
        scenarios = slice(owner * SCN_DEV, (owner + 1) * SCN_DEV)
        for block in range(4):
            columns = slice(block * BLK, (block + 1) * BLK)
            change = wide(finals[owner, block // 2, block % 2])
            for t in range(HOURS):
                new_price[t, scenarios, columns] = (
                    price[t, scenarios, columns] - change[t * SCN_DEV : (t + 1) * SCN_DEV, :]
                )
    new_mult[...] = mult[...]


def finish(finals, price, mult):
    vmem = pl.BlockSpec(memory_space=pltpu.VMEM)
    return pl.pallas_call(
        finish_kernel,
        name="finish",
        out_shape=(jax.ShapeDtypeStruct(price.shape, F32), jax.ShapeDtypeStruct(mult.shape, F32)),
        in_specs=[vmem] * 3,
        out_specs=(vmem, vmem),
        compiler_params=pltpu.CompilerParams(vmem_limit_bytes=VMEM_LIMIT),
    )(finals, price, mult)


def shards(
    bus_price,
    bus_demand,
    multipliers,
    line_limits,
    ptdf_blocks,
    ptdf_pattern,
    gen_bus,
    state_counts,
    transitions,
    state_level,
    state_cost,
):
    price = bus_price.transpose(1, 0, 2)
    finals, mult = network(
        state_counts,
        gen_bus,
        ptdf_pattern,
        transitions.transpose(1, 0, 2),
        state_level,
        state_cost,
        price,
        bus_demand.transpose(1, 0, 2),
        multipliers.transpose(0, 2, 1, 3),
        line_limits,
        ptdf_blocks,
    )
    new_price, new_mult = finish(finals, price, mult)
    return new_mult.transpose(0, 2, 1, 3), new_price.transpose(1, 0, 2)


def solution(mesh):
    in_specs = (
        P(None, None, "bus"),
        P("gen", None, "bus"),
        P(None, "gen", None, "bus"),
        P("bus"),
        P("bus", None, None, None),
        P("bus", None),
        P(("gen", "bus")),
        P(("gen", "bus")),
        P(("gen", "bus"), None, None),
        P(("gen", "bus"), None),
        P(("gen", "bus"), None),
    )
    out_specs = (P(None, "gen", None, "bus"), P(None, None, "bus"))
    return jax.shard_map(shards, mesh=mesh, in_specs=in_specs, out_specs=out_specs, check_vma=False)
```

```python
import functools

import jax
import jax.numpy as jnp
from jax import lax
from jax.experimental import pallas as pl
from jax.experimental.pallas import tpu as pltpu
from jax.sharding import PartitionSpec as P

STATES = 512
SMALL = 256
BIG_DEV = 6
GEN_DEV = 16
BLK = 128
NNZB = 16
HOURS = 12
SCN = 32
SCN_DEV = 4
ROWS = SCN_DEV * HOURS
BUS_DEV = 512
NX, NZ, NGEN = 4, 8, 8
LINE_BLKS = 6
F32, BF16, I32 = jnp.float32, jnp.bfloat16, jnp.int32
MESH = pl.DeviceIdType.MESH
NN = (((1,), (0,)), ((), ()))
NT = (((1,), (1,)), ((), ()))
OFFSET_LANE = (HOURS % 8) * GEN_DEV
VMEM_LIMIT = 58 * 1024 * 1024


def dot(a, b, dims):
    return lax.dot_general(a, b, dims, preferred_element_type=F32)


def split3(value):
    high = value.astype(BF16)
    rest = value - high.astype(F32)
    middle = rest.astype(BF16)
    low = (rest - middle.astype(F32)).astype(BF16)
    return high, middle, low


def plan_steps(
    counts,
    gen_bus,
    pattern,
    trans,
    level,
    cost,
    price,
    out,
    inverse,
    order,
    table_now,
    table_done,
    prices,
    levels,
    costs,
    op_big,
    op_small,
    turned_big,
    turned_small,
    fwd,
    bwd,
    fwd_now,
    bwd_now,
    result,
):
    big_so_far = jnp.int32(0)
    slots = []
    for g in range(GEN_DEV):
        big = (counts[g] > SMALL).astype(I32)
        slots.append(jnp.where(big == 1, big_so_far, GEN_DEV - 1 - (g - big_so_far)))
        big_so_far = big_so_far + big
    for slot in range(GEN_DEV):
        holder = jnp.int32(0)
        for g in range(1, GEN_DEV):
            holder = holder + jnp.where(slots[g] == slot, g, 0)
        order[slot] = holder

    block_ids = lax.broadcasted_iota(I32, (1, NX * NZ * 4), 1)
    for line in range(LINE_BLKS):
        row = jnp.full((1, NX * NZ * 4), LINE_BLKS * NNZB, I32)
        for j in range(NNZB):
            row = jnp.where(block_ids == pattern[line, j], line * NNZB + j, row)
        table_now[line : line + 1, :] = row
    copy_table = pltpu.make_async_copy(table_now, inverse, table_done)
    copy_table.start()

    lane = lax.broadcasted_iota(I32, (1, BLK), 1)
    offset_row = jnp.full((1, BLK), -1, I32)
    sent_offsets = jnp.zeros((1, BLK), F32)
    for slot in range(GEN_DEV):
        offset = lax.rem(gen_bus[order[slot]], BUS_DEV)
        offset_row = jnp.where(lane == slot, offset, offset_row)
        sent_offsets = jnp.where(lane == OFFSET_LANE + slot, offset.astype(F32), sent_offsets)

    onehot = (lax.broadcasted_iota(I32, (BUS_DEV, BLK), 0) == offset_row).astype(BF16)
    pieces = split3(price[...].reshape(HOURS * SCN, BUS_DEV))
    prices[...] = dot(pieces[0], onehot, NN) + dot(pieces[1], onehot, NN) + dot(pieces[2], onehot, NN)

    state_ids = lax.broadcasted_iota(I32, (1, STATES), 1)
    for slot in range(GEN_DEV):
        g = order[slot]
        levels[slot : slot + 1, :] = level[pl.ds(g, 1), :]
        costs[slot : slot + 1, :] = jnp.where(state_ids < counts[g], cost[pl.ds(g, 1), :], 1e4)

    chunk = 256
    for slot in range(GEN_DEV):
        g = order[slot]
        span = STATES if slot < BIG_DEV else SMALL
        table = op_big.at[slot] if slot < BIG_DEV else op_small.at[slot - BIG_DEV]
        targets = [trans[j, pl.ds(g, 1), :span].astype(jnp.int16) for j in range(3)]

        def build(part, carry, targets=targets, span=span, table=table):
            start = pl.multiple_of(part * chunk, chunk)
            ids = (lax.broadcasted_iota(I32, (chunk, span), 0) + start).astype(jnp.int16)
            hits = [jnp.where(target == ids, BF16(1.0), BF16(0.0)) for target in targets]
            table[pl.ds(start, chunk), :] = hits[0] + hits[1] + hits[2]
            return carry

        lax.fori_loop(0, span // chunk, build, 0)

    def span_of(slot):
        return STATES if slot < BIG_DEV else SMALL

    def operator(slot):
        return op_big[slot] if slot < BIG_DEV else op_small[slot - BIG_DEV]

    def turned(slot):
        return turned_big[slot] if slot < BIG_DEV else turned_small[slot - BIG_DEV]

    def turn(slot):
        if slot < BIG_DEV:
            turned_big[slot] = op_big[slot].T
        else:
            turned_small[slot - BIG_DEV] = op_small[slot - BIG_DEV].T

    def hour_price(hour):
        return prices[pl.ds(pl.multiple_of(hour * SCN, SCN), SCN), :]

    def weight(slot, price_now):
        span = span_of(slot)
        return jnp.exp(
            price_now[:, slot : slot + 1] * levels[slot : slot + 1, :span] - costs[slot : slot + 1, :span]
        )

    def unit(value):
        return value * (1.0 / jnp.sum(value, axis=1, keepdims=True))

    def step_forward(slot, price_now):
        raised = dot(fwd_now[slot, :, : span_of(slot)], turned(slot), NN) * weight(slot, price_now)
        state = unit(raised)
        fwd_now[slot, :, : span_of(slot)] = state.astype(BF16)
        return state

    def step_backward(slot, price_now):
        back = dot(bwd_now[slot, :, : span_of(slot)], operator(slot), NN)
        bwd_now[slot, :, : span_of(slot)] = unit(back * weight(slot, price_now)).astype(BF16)
        return back

    first, last = hour_price(0), hour_price(HOURS - 1)
    for slot in range(GEN_DEV):
        span = span_of(slot)
        turn(slot)
        state = unit(weight(slot, first))
        fwd[0, slot, :, :span] = state
        fwd_now[slot, :, :span] = state.astype(BF16)
        bwd[0, slot, :, :span] = jnp.ones((SCN, span), F32)
        bwd_now[slot, :, :span] = unit(weight(slot, last)).astype(BF16)

    def early(k, carry):
        price_f, price_b = hour_price(k), hour_price(HOURS - 1 - k)
        for slot in range(GEN_DEV):
            span = span_of(slot)
            fwd[k, slot, :, :span] = step_forward(slot, price_f)
            bwd[k, slot, :, :span] = step_backward(slot, price_b)
        return carry

    lanes = lax.broadcasted_iota(I32, (SCN, BLK), 1)

    def mean_level(slot, state, back):
        combined = state * back
        span = span_of(slot)
        top = jnp.sum(combined * levels[slot : slot + 1, :span], axis=1, keepdims=True)
        return top / jnp.sum(combined, axis=1, keepdims=True)

    result[0] = jnp.zeros((SCN, BLK), F32)
    result[1] = jnp.broadcast_to(sent_offsets, (SCN, BLK))

    def late(k, carry):
        other = HOURS - 1 - k
        price_f, price_b = hour_price(k), hour_price(other)
        at_k = jnp.zeros((SCN, BLK), F32)
        at_other = jnp.zeros((SCN, BLK), F32)
        lanes_k = lanes - lax.rem(k, 8) * GEN_DEV
        lanes_other = lanes - other * GEN_DEV
        for slot in range(GEN_DEV):
            span = span_of(slot)
            state = step_forward(slot, price_f)
            back = step_backward(slot, price_b)
            at_k = jnp.where(lanes_k == slot, mean_level(slot, state, bwd[other, slot, :, :span]), at_k)
            at_other = jnp.where(lanes_other == slot, mean_level(slot, fwd[other, slot, :, :span], back), at_other)
        result[lax.div(k, 8)] += at_k
        result[0] += at_other
        return carry

    half = HOURS // 2
    lax.fori_loop(1, half, early, 0)
    lax.fori_loop(half, HOURS, late, 0)

    copy_table.wait()
    for owner in range(NGEN):
        rows = slice(owner * SCN_DEV, (owner + 1) * SCN_DEV)
        for part in range(2):
            out[owner, part * SCN_DEV : (part + 1) * SCN_DEV, :] = result[part, rows, :]


def plan_scratch():
    half = HOURS // 2
    return [
        pltpu.VMEM((NGEN, 2 * SCN_DEV, BLK), F32),
        pltpu.SMEM((8, NX * NZ * 4), I32),
        pltpu.SMEM((GEN_DEV,), I32),
        pltpu.VMEM((8, NX * NZ * 4), I32),
        pltpu.SemaphoreType.DMA,
        pltpu.VMEM((HOURS * SCN, BLK), F32),
        pltpu.VMEM((GEN_DEV, STATES), F32),
        pltpu.VMEM((GEN_DEV, STATES), F32),
        pltpu.VMEM((BIG_DEV, STATES, STATES), BF16),
        pltpu.VMEM((GEN_DEV - BIG_DEV, SMALL, SMALL), BF16),
        pltpu.VMEM((BIG_DEV, STATES, STATES), BF16),
        pltpu.VMEM((GEN_DEV - BIG_DEV, SMALL, SMALL), BF16),
        pltpu.VMEM((half, GEN_DEV, SCN, STATES), F32),
        pltpu.VMEM((half, GEN_DEV, SCN, STATES), F32),
        pltpu.VMEM((GEN_DEV, SCN, STATES), BF16),
        pltpu.VMEM((GEN_DEV, SCN, STATES), BF16),
        pltpu.VMEM((2, SCN, BLK), F32),
    ]


class Links:
    def __init__(self, send, recv):
        self.send, self.recv, self.used, self.copies = send, recv, 0, {}
        self.x = lax.div(lax.axis_index("bus"), NZ)
        self.z = lax.rem(lax.axis_index("bus"), NZ)
        self.g = lax.axis_index("gen")

    def xs(self, step):
        return lax.rem(self.x + step + NX, NX)

    def zs(self, step):
        return lax.rem(self.z + step + NZ, NZ)

    def gs(self, step):
        return lax.rem(self.g + step + NGEN, NGEN)

    def along_x(self, step):
        return {"bus": self.xs(step) * NZ + self.z}

    def along_z(self, step):
        return {"bus": self.x * NZ + self.zs(step)}

    def along_gen(self, step):
        return {"gen": self.gs(step)}

    def start(self, key, src, dst, target):
        index = self.used
        self.used += 1
        copy = pltpu.make_async_remote_copy(
            src_ref=src,
            dst_ref=dst,
            send_sem=self.send.at[index],
            recv_sem=self.recv.at[index],
            device_id=target,
            device_id_type=MESH,
        )
        copy.start()
        assert key not in self.copies
        self.copies[key] = copy

    def arrived(self, key):
        self.copies[key].wait_recv()

    def drain(self):
        for copy in self.copies.values():
            copy.wait_send()


def greet(targets):
    barrier = pltpu.get_barrier_semaphore()
    for target in targets:
        pl.semaphore_signal(barrier, inc=1, device_id=target, device_id_type=MESH)
    return functools.partial(pl.semaphore_wait, barrier, len(targets))


def take_turns(*routines):
    waiting = list(routines)
    while waiting:
        for routine in list(waiting):
            if next(routine, "over") == "over":
                waiting.remove(routine)


def gather_z_first(net, buf):
    def block(dx, dz):
        return buf.at[net.xs(dx), net.zs(dz)]

    def pass_on(dz):
        for i in (1, -1, 2):
            net.start(("Ax", i, dz), block(0, dz), block(0, dz), net.along_x(i))

    for dz in (1, -1, 2, -2, 3, -3, 4):
        net.start(("Az", dz), block(0, 0), block(0, 0), net.along_z(dz))
    pass_on(0)
    yield
    for group in ((1, -1), (2, -2), (3, -3), (4,)):
        for dz in group:
            net.arrived(("Az", dz))
            pass_on(-dz)
        yield
    for dz in (0, -1, 1, -2, 2, -3, 3, -4):
        for i in (1, -1, 2):
            net.arrived(("Ax", i, dz))


def gather_x_first(net, buf):
    def block(dx, dz):
        return buf.at[net.xs(dx), net.zs(dz)]

    def first(dx):
        for i in (2, -2, 1, -1):
            net.start(("Bz", dx, i), block(dx, 0), block(dx, 0), net.along_z(i))

    def second(dx):
        for i in (2, -2):
            near = i // 2
            c = 0 if i > 0 else 1
            net.arrived(("Bz", dx, i))
            net.start(("Bz4", dx, i), block(dx, -i).at[c], block(dx, -i).at[c], net.along_z(i))
            net.start(("Bz3", dx, i), block(dx, -i), block(dx, -i), net.along_z(near))

    for i in (2, 1, -1):
        net.start(("Bx", i), block(0, 0), block(0, 0), net.along_x(i))
    first(0)
    yield
    for i in (-1, 1, 2):
        net.arrived(("Bx", i))
        first(-i)
    yield
    second(0)
    yield
    second(1)
    second(-1)
    yield
    second(-2)
    yield
    for dx in (0, 1, -1, -2):
        for i in (1, -1):
            net.arrived(("Bz", dx, i))
        for i in (2, -2):
            net.arrived(("Bz3", dx, i))
            net.arrived(("Bz4", dx, i))


def wide(value):
    return value.astype(F32)


def reduce_x_first(net, part, along_x, to_z, arrived, kept, final):
    far_first = (4, 3, 5, 2, 6, 1, 7, 0)
    for dz in far_first:
        for n, i in enumerate((2, 1, -1)):
            net.start(("sum Ax", n, dz), part.at[net.xs(i), net.zs(dz)], along_x.at[n, dz], net.along_x(i))
    yield
    yield
    for dz in far_first:
        value = wide(part[net.x, net.zs(dz)])
        for n in range(3):
            net.arrived(("sum Ax", n, dz))
            value = value + wide(along_x[n, dz])
        if dz:
            to_z[dz] = value.astype(BF16)
            net.start(("sum Az", dz), to_z.at[dz], arrived.at[dz], net.along_z(dz))
        else:
            kept[...] = value
        if dz in (5, 6):
            yield
    yield
    value = kept[...]
    for dz in (1, 7, 2, 6, 3, 5, 4):
        net.arrived(("sum Az", dz))
        value = value + wide(arrived[dz])
    final[...] = value.astype(BF16)
    yield from spread_result(net, 0)


def reduce_z_first(net, part, near, third, fourth, to_two, from_two, to_x, arrived, kept, final):
    columns = (2, 1, 3, 0)
    for dx in columns:
        column = net.xs(dx)
        for n, i in enumerate((1, -1)):
            net.start(("sum B4", dx, n), part.at[column, net.zs(4), n], fourth.at[dx, n], net.along_z(2 * i))
            net.start(("sum B3", dx, n), part.at[column, net.zs(3 * i)], third.at[dx, n], net.along_z(i))
    for dx in columns:
        for n, i in enumerate((1, -1)):
            net.start(("sum B1", dx, n), part.at[net.xs(dx), net.zs(i)], near.at[dx, n], net.along_z(i))
    yield
    for dx in columns:
        for n, i in enumerate((1, -1)):
            net.arrived(("sum B3", dx, n))
            net.arrived(("sum B4", dx, n))
            value = wide(part[net.xs(dx), net.zs(2 * i)]) + wide(third[dx, n])
            to_two[dx, n, 1 - n] = value[1 - n].astype(BF16)
            to_two[dx, n, n] = (value[n] + wide(fourth[dx, n])).astype(BF16)
            net.start(("sum B2", dx, n), to_two.at[dx, n], from_two.at[dx, n], net.along_z(2 * i))
        if dx in (2, 3):
            yield
    yield
    for dx in columns:
        value = wide(part[net.xs(dx), net.z])
        for n in range(2):
            net.arrived(("sum B1", dx, n))
            net.arrived(("sum B2", dx, n))
            value = value + (wide(near[dx, n]) + wide(from_two[dx, n]))
        if dx:
            to_x[dx] = value.astype(BF16)
            net.start(("sum Bx", dx), to_x.at[dx], arrived.at[dx], net.along_x(dx))
        else:
            kept[...] = value
    yield
    value = kept[...]
    for dx in (1, 3, 2):
        net.arrived(("sum Bx", dx))
        value = value + wide(arrived[dx])
    final[...] = value.astype(BF16)
    yield from spread_result(net, 1)


def spread_result(net, half):
    for i in range(1, NGEN):
        mine = net.finals.at[net.g, half]
        net.start(("out", half, i), mine, mine, net.along_gen(i))
    yield


NET_COPIES = 7 + 31 + 35 + 31 + 35 + 14


def place_of(block):
    device, c = lax.div(block, 4), lax.rem(block, 4)
    return (lax.div(c, 2) * (NX * NZ) + device) * 2 + lax.rem(c, 2)


def network_kernel(
    counts,
    gen_bus,
    pattern,
    trans,
    level,
    cost,
    price,
    demand,
    mult,
    limits,
    ptdf_far,
    finals,
    new_mult,
    peers,
    netf,
    nets,
    ptdf,
    changes,
    spreads,
    shares,
    a_x,
    a_to_z,
    a_arrived,
    a_kept,
    b_near,
    b_third,
    b_fourth,
    b_to_two,
    b_from_two,
    b_to_x,
    b_arrived,
    b_kept,
    send,
    recv,
    done,
    *plan_refs,
):
    net = Links(send, recv)
    net.finals = finals
    load_ptdf = pltpu.make_async_copy(ptdf_far, ptdf, done)
    load_ptdf.start()
    everyone_here = greet(
        [net.along_x(i) for i in range(1, NX)]
        + [net.along_z(i) for i in range(1, NZ)]
        + [net.along_gen(i) for i in range(1, NGEN)]
    )
    generation, inverse = plan_refs[0], plan_refs[1]
    plan_steps(counts, gen_bus, pattern, trans, level, cost, price, *plan_refs)
    everyone_here()

    for i in range(1, NGEN):
        net.start(("gen", i), generation.at[net.gs(i)], peers.at[net.g], net.along_gen(i))
    peers[net.g] = generation[net.g]
    for i in range(1, NGEN):
        net.arrived(("gen", i))
    lane_group = lax.div(lax.broadcasted_iota(I32, (2 * SCN_DEV, BLK), 1), GEN_DEV)
    by_hour = [jnp.zeros((2 * SCN_DEV, BLK), F32) for hour in range(8)]
    for source in range(NGEN):
        packed = peers[source]
        for hour in range(8):
            moved = pltpu.roll(packed, (source - hour) % NGEN * GEN_DEV, 1) if source != hour else packed
            by_hour[hour] = jnp.where(lane_group == source, moved, by_hour[hour])
    hours = [by_hour[t % 8][t // 8 * SCN_DEV : (t // 8 + 1) * SCN_DEV, :] for t in range(HOURS)]
    offsets = by_hour[HOURS % 8][SCN_DEV : SCN_DEV + 1, :]
    total = jnp.concatenate(hours, axis=0)

    spots = wide(lax.broadcasted_iota(I32, (BUS_DEV, BLK), 0))
    onehot = (spots == offsets).astype(BF16)
    high, middle, low = split3(total)
    netf[...] = dot(high, onehot, NT) + dot(middle, onehot, NT) + dot(low, onehot, NT)
    for t in range(HOURS):
        netf[t * SCN_DEV : (t + 1) * SCN_DEV, :] -= demand[t]
    rounded = netf[...].astype(BF16)
    for half in range(2):
        for c in range(2):
            column = (half * 2 + c) * BLK
            nets[half, net.x, net.z, c] = rounded[:, column : column + BLK]

    take_turns(gather_x_first(net, nets.at[1]), gather_z_first(net, nets.at[0]))

    load_ptdf.wait()
    blocks = nets.reshape(2 * NX * NZ * 2, ROWS, BLK)
    spreads[LINE_BLKS * NNZB] = jnp.zeros((ROWS, BLK), F32)
    for line in range(LINE_BLKS):
        lanes = slice(line * BLK, (line + 1) * BLK)
        places = [place_of(pattern[line, j]) for j in range(NNZB)]
        flow = jnp.zeros((ROWS, BLK), F32)
        for j in range(0, NNZB, 2):
            pair = jnp.concatenate([blocks[places[j]], blocks[places[j + 1]]], axis=1)
            flow = flow + dot(pair, ptdf[line, j : j + 2].reshape(2 * BLK, BLK), NN)
        limit = limits[lanes].reshape(1, BLK)
        for t in range(HOURS):
            rows = slice(t * SCN_DEV, (t + 1) * SCN_DEV)
            here = flow[rows, :]
            upper_old, lower_old = mult[0, t, :, lanes], mult[1, t, :, lanes]
            upper = jnp.maximum(0.0, upper_old + (here - limit))
            lower = jnp.maximum(0.0, lower_old + (-here - limit))
            new_mult[0, t, :, lanes] = upper
            new_mult[1, t, :, lanes] = lower
            changes[rows, :] = (upper - upper_old) - (lower - lower_old)
        change = changes[...].astype(BF16)
        spread = dot(change, ptdf[line].reshape(NNZB * BLK, BLK), NT)
        for j in range(NNZB):
            spreads[line * NNZB + j] = spread[:, j * BLK : (j + 1) * BLK]

    def collect(half, device, carry):
        x, z = lax.div(device, NZ), lax.rem(device, NZ)
        for c in range(2):
            block = device * 4 + half * 2 + c
            value = spreads[inverse[0, block]]
            for line in range(1, LINE_BLKS):
                value = value + spreads[inverse[line, block]]
            shares[half, x, z, c] = value.astype(BF16)
        return carry

    lax.fori_loop(0, NX * NZ, functools.partial(collect, 1), 0)
    longer = reduce_z_first(
        net,
        shares.at[1],
        b_near,
        b_third,
        b_fourth,
        b_to_two,
        b_from_two,
        b_to_x,
        b_arrived,
        b_kept,
        finals.at[net.g, 1],
    )
    next(longer)
    lax.fori_loop(0, NX * NZ, functools.partial(collect, 0), 0)
    shorter = reduce_x_first(net, shares.at[0], a_x, a_to_z, a_arrived, a_kept, finals.at[net.g, 0])
    next(shorter)
    take_turns(longer, shorter)
    for half in range(2):
        for i in range(1, NGEN):
            net.arrived(("out", half, i))
    net.drain()


def network(counts, gen_bus, pattern, trans, level, cost, price, demand, mult, limits, ptdf):
    vmem = pl.BlockSpec(memory_space=pltpu.VMEM)
    smem = pl.BlockSpec(memory_space=pltpu.SMEM)
    far = pl.BlockSpec(memory_space=pl.ANY)
    piece = (2, ROWS, BLK)
    everything = (2, NX, NZ) + piece
    return pl.pallas_call(
        network_kernel,
        name="network",
        out_shape=(
            jax.ShapeDtypeStruct((NGEN, 2) + piece, BF16),
            jax.ShapeDtypeStruct(mult.shape, F32),
        ),
        in_specs=[smem] * 3 + [vmem] * 7 + [far],
        out_specs=(vmem, vmem),
        scratch_shapes=[
            pltpu.VMEM((NGEN, 2 * SCN_DEV, BLK), F32),
            pltpu.VMEM((ROWS, BUS_DEV), F32),
            pltpu.VMEM(everything, BF16),
            pltpu.VMEM(ptdf.shape, BF16),
            pltpu.VMEM((ROWS, BLK), F32),
            pltpu.VMEM((LINE_BLKS * NNZB + 1, ROWS, BLK), F32),
            pltpu.VMEM(everything, BF16),
            pltpu.VMEM((3, NZ) + piece, BF16),
            pltpu.VMEM((NZ,) + piece, BF16),
            pltpu.VMEM((NZ,) + piece, BF16),
            pltpu.VMEM(piece, F32),
            pltpu.VMEM((NX, 2) + piece, BF16),
            pltpu.VMEM((NX, 2) + piece, BF16),
            pltpu.VMEM((NX, 2, ROWS, BLK), BF16),
            pltpu.VMEM((NX, 2) + piece, BF16),
            pltpu.VMEM((NX, 2) + piece, BF16),
            pltpu.VMEM((NX,) + piece, BF16),
            pltpu.VMEM((NX,) + piece, BF16),
            pltpu.VMEM(piece, F32),
            pltpu.SemaphoreType.DMA((NET_COPIES,)),
            pltpu.SemaphoreType.DMA((NET_COPIES,)),
            pltpu.SemaphoreType.DMA,
        ]
        + plan_scratch(),
        compiler_params=pltpu.CompilerParams(
            collective_id=0, has_side_effects=True, vmem_limit_bytes=VMEM_LIMIT
        ),
    )(counts, gen_bus, pattern, trans, level, cost, price, demand, mult, limits, ptdf)


def finish_kernel(finals, price, mult, new_price, new_mult):
    for owner in range(NGEN):
        scenarios = slice(owner * SCN_DEV, (owner + 1) * SCN_DEV)
        for block in range(4):
            columns = slice(block * BLK, (block + 1) * BLK)
            change = wide(finals[owner, block // 2, block % 2])
            for t in range(HOURS):
                new_price[t, scenarios, columns] = (
                    price[t, scenarios, columns] - change[t * SCN_DEV : (t + 1) * SCN_DEV, :]
                )
    new_mult[...] = mult[...]


def finish(finals, price, mult):
    vmem = pl.BlockSpec(memory_space=pltpu.VMEM)
    return pl.pallas_call(
        finish_kernel,
        name="finish",
        out_shape=(jax.ShapeDtypeStruct(price.shape, F32), jax.ShapeDtypeStruct(mult.shape, F32)),
        in_specs=[vmem] * 3,
        out_specs=(vmem, vmem),
        compiler_params=pltpu.CompilerParams(vmem_limit_bytes=VMEM_LIMIT),
    )(finals, price, mult)


def shards(
    bus_price,
    bus_demand,
    multipliers,
    line_limits,
    ptdf_blocks,
    ptdf_pattern,
    gen_bus,
    state_counts,
    transitions,
    state_level,
    state_cost,
):
    price = bus_price.transpose(1, 0, 2)
    finals, mult = network(
        state_counts,
        gen_bus,
        ptdf_pattern,
        transitions.transpose(1, 0, 2),
        state_level,
        state_cost,
        price,
        bus_demand.transpose(1, 0, 2),
        multipliers.transpose(0, 2, 1, 3),
        line_limits,
        ptdf_blocks,
    )
    new_price, new_mult = finish(finals, price, mult)
    return new_mult.transpose(0, 2, 1, 3), new_price.transpose(1, 0, 2)


def solution(mesh):
    in_specs = (
        P(None, None, "bus"),
        P("gen", None, "bus"),
        P(None, "gen", None, "bus"),
        P("bus"),
        P("bus", None, None, None),
        P("bus", None),
        P(("gen", "bus")),
        P(("gen", "bus")),
        P(("gen", "bus"), None, None),
        P(("gen", "bus"), None),
        P(("gen", "bus"), None),
    )
    out_specs = (P(None, "gen", None, "bus"), P(None, None, "bus"))
    return jax.shard_map(shards, mesh=mesh, in_specs=in_specs, out_specs=out_specs, check_vma=False)
```
